32 devices in a mesh: tile: 32 (over z, y, x, core), lev: 1.
Axes of the slice: x: 2, y: 2, z: 4, core: 2. Of those that a mesh axis runs over, the one named last changes fastest.
Arguments:
- cotangent: float32 [24, 4, 64, 900], P('lev', None, 'tile'), may hold values from -6 to 6
- courant_x: float32 [24, 64, 900], P('lev', 'tile'), may hold values from -0.6 to 0.6
- courant_y: float32 [24, 64, 900], P('lev', 'tile'), may hold values from -0.6 to 0.6
- diffusivity: float32 [64, 900], P('tile'), may hold values from 0.04 to 0.16
- vert_diff: float32 [24, 64, 900], P('lev', 'tile'), may hold values from 0.5 to 2000
- level_count: int32 [64, 900], P('tile'), may hold values from 0 to 24
- edge_tile: int32 [64, 4], P('tile'), may hold values from -1 to 63, as said below
- edge_code: int32 [64, 4], P('tile'), may hold values from 0 to 7
- corner_tile: int32 [64, 4], P('tile'), may hold values from -1 to 63, as said below
- corner_code: int32 [64, 4], P('tile'), may hold values from 0 to 3
Outputs:
- tracer_adjoint: float32 [24, 4, 64, 900], P('lev', None, 'tile')
The draws below stay inside these ranges and needn't reach their ends.
Inputs may be any that keep to these rules, and one draw needn't show every extreme that they name: Side lists are symmetric: if edge_tile[t, s] = q and edge_code[t, s] = e + 4 r, then edge_tile[q, e] = t and edge_code[q, e] = s + 4 r. Every partner q satisfies min(|q - t|, 64 - |q - t|) <= 16. Sides at the band's rim and sides towards land are -1. Corner lists are symmetric: if corner_tile[t, c] = q and corner_code[t, c] = k, then corner_tile[q, k] = t and corner_code[q, k] = c. Every partner q satisfies min(|q - t|, 64 - |q - t|) <= 16.
All inputs are finite; a program needn't handle non-finite values.
Results may differ from the reference program's by a relative error of at most 0.0003.
Values sent between devices are 32-bit elements; how exact they have to be, the bound alone decides.
A program may use at most 128 MiB of HBM per device.

```python
import math
import jax
import jax.numpy as jnp
from jax import lax

EDGE = 30
CELLS = 900
TRACERS = 4
LEV_DEV = 24
LEVELS = 24
TILES = 64
BAND = 8
ALONG = 10
LAND = 16


def build_lists(key):
    folded = jax.random.fold_in(key, 7)
    key_land, key_seam = jax.random.split(folded)
    positions = ALONG * BAND
    shuffled = jax.random.permutation(key_land, positions)
    land_flag = jnp.zeros((positions,), jnp.int32).at[shuffled[:LAND]].set(1)
    wet_index = jnp.where(land_flag == 0, jnp.cumsum(1 - land_flag) - 1, -1).astype(jnp.int32)
    wet_place = jnp.argsort(land_flag, stable=True)[:TILES].astype(jnp.int32)
    column = wet_place // BAND
    across = wet_place % BAND
    seam_flags = jax.random.randint(key_seam, (ALONG,), 0, 2).astype(jnp.int32)

    def lookup(column_to, across_to, inside):
        grid_spot = column_to % ALONG * BAND + jnp.clip(across_to, 0, BAND - 1)
        wet_found = wet_index[grid_spot]
        return jnp.where(inside & (wet_found >= 0), wet_found, -1).astype(jnp.int32)
    always = across >= 0
    south_tile = lookup(column, across - 1, across > 0)
    north_tile = lookup(column, across + 1, across < BAND - 1)
    west_seam = seam_flags[(column - 1) % ALONG]
    west_tile = lookup(column - 1, jnp.where(west_seam == 1, BAND - 1 - across, across), always)
    east_seam = seam_flags[column % ALONG]
    east_tile = lookup(column + 1, jnp.where(east_seam == 1, BAND - 1 - across, across), always)
    edge_tiles = jnp.stack([south_tile, north_tile, west_tile, east_tile], axis=1)
    edge_codes = jnp.stack([jnp.ones_like(across), jnp.zeros_like(across), 3 + 4 * west_seam, 2 + 4 * east_seam], axis=1).astype(jnp.int32)
    corner_tiles = []
    corner_codes = []
    for corner_slot in range(4):
        row_bit = corner_slot // 2
        col_bit = corner_slot % 2
        seam_here = seam_flags[(column + col_bit - 1) % ALONG]
        target = across + 2 * row_bit - 1
        inside = (target >= 0) & (target < BAND)
        across_to = jnp.where(seam_here == 1, BAND - 1 - target, target)
        corner_tiles.append(lookup(column + 2 * col_bit - 1, across_to, inside))
        corner_codes.append(jnp.where(seam_here == 1, 2 * row_bit + 1 - col_bit, 3 - corner_slot).astype(jnp.int32))
    return (edge_tiles, edge_codes, jnp.stack(corner_tiles, axis=1), jnp.stack(corner_codes, axis=1))


def draw_edge_tile(key, part):
    return build_lists(key)[0]


def draw_edge_code(key, part):
    return build_lists(key)[1]


def draw_corner_tile(key, part):
    return build_lists(key)[2]


def draw_corner_code(key, part):
    return build_lists(key)[3]


def draw_vert_diff(key, part):
    folded = jax.random.fold_in(key, 11)
    key_base, key_strong, key_pick, key_depth = jax.random.split(folded, 4)
    base_values = jnp.exp(jax.random.uniform(key_base, (LEVELS, TILES, CELLS), jnp.float32, jnp.log(0.5), jnp.log(20.0)))
    strong_values = jnp.exp(jax.random.uniform(key_strong, (LEVELS, TILES, CELLS), jnp.float32, jnp.log(100.0), jnp.log(2000.0)))
    share = 0.34
    shallowest = LEV_DEV // 2 + 1
    picked = jax.random.uniform(key_pick, (TILES, CELLS), jnp.float32) < share
    mixed_depth = jax.random.randint(key_depth, (TILES, CELLS), shallowest, LEVELS + 1)
    level_index = jnp.arange(LEVELS, dtype=jnp.int32)[:, None, None]
    inside = picked[None] & (level_index < mixed_depth[None])
    return jnp.where(inside, strong_values, base_values).astype(jnp.float32)


def plant(drawn, own_key, low, high):
    spot = [jax.random.randint(jax.random.fold_in(own_key, axis), (), 0, length) for axis, length in enumerate(drawn.shape)]
    main_axis = drawn.shape.index(max(drawn.shape))
    beside = spot[:main_axis] + [(spot[main_axis] + 1) % drawn.shape[main_axis]] + spot[main_axis + 1:]
    return drawn.at[tuple(spot)].set(low).at[tuple(beside)].set(high)


def block_scale(own_key, extent, pieces, least, largest):
    def one(dim, shards_of):
        draws = jax.random.uniform(jax.random.fold_in(jax.random.fold_in(own_key, 6), dim), (shards_of,), jnp.float32, least / len(pieces), largest / len(pieces))
        return jnp.repeat(jnp.exp(draws), extent[dim] // shards_of).reshape((-1,) + (1,) * (len(extent) - dim - 1))

    gain = one(*pieces[0])
    for cut in pieces[1:]:
        gain = gain * one(*cut)
    return gain


def centred(stream_key, shape, deviation, limit, cuts=(), held_as=jnp.bfloat16):
    level = block_scale(stream_key, shape, cuts, -0.22, 0.18) if cuts else 1.0
    result = jax.random.normal(stream_key, shape, jnp.float32) * deviation * level
    return jnp.minimum(jnp.maximum(result, -limit), limit).astype(held_as)


def setup_inputs(seed: int = 0) -> dict:
    seeds = jax.random.split(jax.random.key(seed), 11)
    return {
        "cotangent": centred(seeds[0], (LEVELS, TRACERS, TILES, CELLS), 1.0, 6.0, ((2, 32),), jnp.float32),
        "courant_x": centred(seeds[1], (LEVELS, TILES, CELLS), 0.2, 0.6, ((1, 32),), jnp.float32),
        "courant_y": centred(seeds[2], (LEVELS, TILES, CELLS), 0.2, 0.6, ((1, 32),), jnp.float32),
        "diffusivity": jnp.clip(jnp.exp(math.log(0.16) - 1.3862944 * jax.random.uniform(seeds[3], (TILES, CELLS), jnp.float32) ** block_scale(seeds[3], (TILES, CELLS), ((0, 32),), -0.2, 0.2)), 0.04, 0.16),
        "vert_diff": draw_vert_diff(jax.random.fold_in(seeds[10], 71), 0),
        "level_count": plant(jax.random.randint(seeds[5], (TILES, CELLS), 0, LEVELS + 1), jax.random.fold_in(seeds[5], 1), 0, LEVELS).astype(jnp.int32),
        "edge_tile": draw_edge_tile(jax.random.fold_in(seeds[10], 71), 0),
        "edge_code": draw_edge_code(jax.random.fold_in(seeds[10], 71), 0),
        "corner_tile": draw_corner_tile(jax.random.fold_in(seeds[10], 71), 0),
        "corner_code": draw_corner_code(jax.random.fold_in(seeds[10], 71), 0),
    }


stencil_offsets = [(0, -1), (0, 1), (-1, 0), (1, 0), (-1, -1), (-1, 1), (1, -1), (1, 1)]

def stencil_weights(diffuse, flow_x, flow_y):
    return [diffuse + 0.5 * flow_x, diffuse - 0.5 * flow_x, diffuse + 0.5 * flow_y, diffuse - 0.5 * flow_y, 0.25 * diffuse, 0.25 * diffuse, 0.25 * diffuse, 0.25 * diffuse]

def eliminate(right_side, coupling_up, coupling_down, initial):

    def advance(state, inputs):
        factor, partial_value = state
        source, upper_term, lower_term = inputs
        divisor = 1.0 + upper_term + lower_term + upper_term * factor
        factor_new = -lower_term / divisor
        partial_new = (source + upper_term * partial_value) / divisor
        return ((factor_new, partial_new), (factor_new, partial_new))
    final_state, outputs = lax.scan(advance, initial, (right_side, coupling_up, coupling_down))
    return outputs

def substitute(factors, partials, below_field):

    def backward(state, inputs):
        factor, partial_value = inputs
        column_value = partial_value - factor * state
        return (column_value, column_value)
    final_state, fields = lax.scan(backward, below_field, (factors, partials), reverse=True)
    return fields

def extend(square, edge_tile, edge_code, corner_tile, corner_code):
    strips = jnp.stack([square[:, :, 0, :], square[:, :, -1, :], square[:, :, :, 0], square[:, :, :, -1]], axis=2)
    corner_cells = jnp.stack([square[:, :, 0, 0], square[:, :, 0, -1], square[:, :, -1, 0], square[:, :, -1, -1]], axis=2)
    safe_edge = jnp.maximum(edge_tile, 0)
    fetched = strips[:, safe_edge, edge_code % 4]
    fetched = jnp.where((edge_code >= 4)[None, :, :, None], fetched[..., ::-1], fetched)
    fetched = fetched * (edge_tile >= 0).astype(jnp.float32)[None, :, :, None]
    safe_corner = jnp.maximum(corner_tile, 0)
    corner_values = corner_cells[:, safe_corner, corner_code] * (corner_tile >= 0).astype(jnp.float32)[None]
    padded = jnp.pad(square, ((0, 0), (0, 0), (1, 1), (1, 1)))
    padded = padded.at[:, :, 0, 1:-1].set(fetched[:, :, 0])
    padded = padded.at[:, :, -1, 1:-1].set(fetched[:, :, 1])
    padded = padded.at[:, :, 1:-1, 0].set(fetched[:, :, 2])
    padded = padded.at[:, :, 1:-1, -1].set(fetched[:, :, 3])
    padded = padded.at[:, :, 0, 0].set(corner_values[:, :, 0])
    padded = padded.at[:, :, 0, -1].set(corner_values[:, :, 1])
    padded = padded.at[:, :, -1, 0].set(corner_values[:, :, 2])
    padded = padded.at[:, :, -1, -1].set(corner_values[:, :, 3])
    return padded

def reference(cotangent, courant_x, courant_y, diffusivity, vert_diff, level_count, edge_tile, edge_code, corner_tile, corner_code):
    depth_index = jnp.arange(LEVELS, dtype=jnp.int32)[:, None, None]
    wet_mask = (depth_index < level_count[None]).astype(jnp.float32)
    coupling = jnp.where(depth_index == 0, jnp.float32(0.0), vert_diff * wet_mask)
    lower = jnp.concatenate([coupling[1:], jnp.zeros_like(coupling[:1])], axis=0)
    diffuse = diffusivity.reshape(1, TILES, EDGE, EDGE)
    flow_x = courant_x.reshape(LEVELS, TILES, EDGE, EDGE)
    flow_y = courant_y.reshape(LEVELS, TILES, EDGE, EDGE)
    weights = stencil_weights(diffuse, flow_x, flow_y)

    def forward(field):
        masked = (field * wet_mask).reshape(LEVELS, TILES, EDGE, EDGE)
        padded = extend(masked, edge_tile, edge_code, corner_tile, corner_code)
        combined = (1.0 - 5.0 * diffuse) * masked
        for (shift_row, shift_col), weight in zip(stencil_offsets, weights):
            combined = combined + weight * padded[:, :, 1 + shift_row:1 + shift_row + EDGE, 1 + shift_col:1 + shift_col + EDGE]
        mixed = combined.reshape(LEVELS, TILES, CELLS) * wet_mask
        initial = (jnp.zeros((TILES, CELLS), jnp.float32), jnp.zeros((TILES, CELLS), jnp.float32))
        factors, partials = eliminate(mixed, coupling, lower, initial)
        return substitute(factors, partials, jnp.zeros((TILES, CELLS), jnp.float32))
    primal_out, pullback = jax.vjp(forward, jnp.zeros((LEVELS, TILES, CELLS), jnp.float32))
    per_tracer = jnp.moveaxis(cotangent, 1, 0)
    adjoint = lax.map(lambda tracer_seed: pullback(tracer_seed)[0], per_tracer)
    return jnp.moveaxis(adjoint, 0, 1)
```

```python
import functools

import jax
import jax.numpy as jnp
import numpy as np
from jax import lax
from jax.experimental import pallas as pl
from jax.experimental.pallas import tpu as pltpu
from jax.sharding import PartitionSpec as P

EDGE = 30
BAND = 8


stencil_offsets = [(0, -1), (0, 1), (-1, 0), (1, 0), (-1, -1), (-1, 1), (1, -1), (1, 1)]


def from_behind(value, axis, steps):
    count = lax.axis_size(axis)
    initial, last = (max(0, -steps), min(count, count - steps))
    return lax.ppermute(value, axis, [(source, source + steps) for source in range(initial, last)])


def shifted_2(value, axis, by):
    devices = lax.axis_size(axis)
    return lax.ppermute(value, axis, [(i, (i + by) % devices) for i in range(devices)])


def stencil_weights(diffuse, flow_x, flow_y):
    return [
        diffuse + 0.5 * flow_x,
        diffuse - 0.5 * flow_x,
        diffuse + 0.5 * flow_y,
        diffuse - 0.5 * flow_y,
        0.25 * diffuse,
        0.25 * diffuse,
        0.25 * diffuse,
        0.25 * diffuse,
    ]


def eliminate(right_side, coupling_up, coupling_down, initial):

    def advance(state, inputs):
        factor, partial_value = state
        source, upper_term, lower_term = inputs
        divisor = 1.0 + upper_term + lower_term + upper_term * factor
        factor_new = -lower_term / divisor
        partial_new = (source + upper_term * partial_value) / divisor
        return ((factor_new, partial_new), (factor_new, partial_new))

    final_state, outputs = lax.scan(advance, initial, (right_side, coupling_up, coupling_down))
    return outputs


def substitute(factors, partials, below_field):

    def backward(state, inputs):
        factor, partial_value = inputs
        column_value = partial_value - factor * state
        return (column_value, column_value)

    final_state, fields = lax.scan(backward, below_field, (factors, partials), reverse=True)
    return fields


def placing_table():
    cells = []
    for border in range(4):
        for position in range(EDGE):
            cells.append(
                [position, (EDGE - 1) * EDGE + position, position * EDGE, position * EDGE + EDGE - 1][border]
            )
    cells += [0, EDGE - 1, (EDGE - 1) * EDGE, EDGE * EDGE - 1]
    placing = np.zeros((len(cells), EDGE * EDGE), np.float32)
    placing[np.arange(len(cells)), np.array(cells)] = 1.0
    return placing


def embed(field):
    leading = field.shape[:-1]
    square = field.reshape(leading + (EDGE, EDGE))
    padded = jnp.pad(square, [(0, 0)] * len(leading) + [(1, 1), (1, 1)])
    return padded.reshape(leading + ((EDGE + 2) * (EDGE + 2),))


def shards(
    cotangent,
    courant_x,
    courant_y,
    diffusivity,
    vert_diff,
    level_count,
    edge_tile,
    edge_code,
    corner_tile,
    corner_code,
):
    levels_here = cotangent.shape[0]
    tracers = cotangent.shape[1]
    tiles_here = cotangent.shape[2]
    cells = cotangent.shape[3]
    padded_edge = EDGE + 2
    cycle_size = 4 * EDGE + 4
    lev_count = lax.axis_size("lev")
    depth_index = (
        lax.axis_index("lev") * levels_here
        + jnp.arange(levels_here, dtype=jnp.int32)[:, None, None]
    )
    wet_mask = (depth_index < level_count[None]).astype(jnp.float32)
    coupling = jnp.where(depth_index == 0, jnp.float32(0.0), vert_diff * wet_mask)
    deeper = from_behind(coupling[0], "lev", -1)
    coupling_down = jnp.concatenate([coupling[1:], deeper[None]], axis=0)[:, None]
    coupling_up = coupling[:, None]
    initial = (
        jnp.zeros((1, tiles_here, cells), jnp.float32),
        jnp.zeros((tracers, tiles_here, cells), jnp.float32),
    )
    for sweep_index in range(lev_count - 1):
        factors, partials = eliminate(cotangent, coupling_up, coupling_down, initial)
        initial = from_behind((factors[-1], partials[-1]), "lev", 1)
    factors, partials = eliminate(cotangent, coupling_up, coupling_down, initial)
    below_field = jnp.zeros((tracers, tiles_here, cells), jnp.float32)
    for sweep_index in range(lev_count - 1):
        fields = substitute(factors, partials, below_field)
        below_field = from_behind(fields[0], "lev", -1)
    solved = substitute(factors, partials, below_field)
    weighted = solved * wet_mask[:, None]
    weighted_ext = embed(weighted)
    diffuse_ext = embed(diffusivity)[None, None]
    flow_x_ext = embed(courant_x)[:, None]
    flow_y_ext = embed(courant_y)[:, None]
    weights = stencil_weights(diffuse_ext, flow_x_ext, flow_y_ext)
    leading = weighted_ext.shape[:-1]
    spread = jnp.zeros_like(weighted_ext)
    for (shift_row, shift_col), weight in zip(stencil_offsets, weights):
        contribution = weight * weighted_ext
        offset = shift_row * padded_edge + shift_col
        if offset > 0:
            shifted = jnp.concatenate(
                [jnp.zeros(leading + (offset,), jnp.float32), contribution[..., :-offset]], axis=-1
            )
        else:
            shifted = jnp.concatenate(
                [contribution[..., -offset:], jnp.zeros(leading + (-offset,), jnp.float32)], axis=-1
            )
        spread = spread + shifted
    placing = placing_table()
    framed = spread.reshape(leading + (padded_edge, padded_edge))
    outgoing = jnp.concatenate(
        [
            framed[..., 0, 1:-1],
            framed[..., -1, 1:-1],
            framed[..., 1:-1, 0],
            framed[..., 1:-1, -1],
            framed[..., 0, :1],
            framed[..., 0, -1:],
            framed[..., -1, :1],
            framed[..., -1, -1:],
        ],
        axis=-1,
    )
    interior = spread.reshape(leading + (padded_edge, padded_edge))[..., 1:-1, 1:-1].reshape(
        solved.shape
    )
    partners = jnp.concatenate([edge_tile, corner_tile], axis=1)

    def collect(gathered_sum, portion, first_tile):
        tile_span = portion.shape[2]
        onehot = (
            partners[:, :, None]
            == first_tile + jnp.arange(tile_span, dtype=jnp.int32)[None, None, :]
        ).astype(jnp.float32)
        return gathered_sum + jnp.einsum(
            "tkw,dnwr->dntkr", onehot, portion, precision=lax.Precision.HIGHEST
        )

    tile_count = lax.axis_size("tile")
    own_index = lax.axis_index("tile")
    reach = (2 * BAND + tiles_here - 1) // tiles_here
    fetched = collect(
        jnp.zeros((levels_here, tracers, tiles_here, 8, cycle_size), jnp.float32),
        outgoing,
        own_index * tiles_here,
    )
    for distance in range(-reach, reach + 1):
        if distance != 0:
            portion = shifted_2(outgoing, "tile", distance)
            source = (own_index - distance) % tile_count
            fetched = collect(fetched, portion, source * tiles_here)
    side_values = fetched[:, :, :, :4, : 4 * EDGE].reshape(
        levels_here, tracers, tiles_here, 4, 4, EDGE
    )
    side_choice = (
        (edge_code % 4)[:, :, None] == jnp.arange(4, dtype=jnp.int32)[None, None, :]
    ).astype(jnp.float32)
    strips = jnp.sum(side_values * side_choice[None, None, :, :, :, None], axis=4)
    strips = jnp.where((edge_code >= 4)[None, None, :, :, None], strips[..., ::-1], strips)
    corner_values = fetched[:, :, :, 4:, 4 * EDGE :]
    corner_choice = (
        corner_code[:, :, None] == jnp.arange(4, dtype=jnp.int32)[None, None, :]
    ).astype(jnp.float32)
    corner_picked = jnp.sum(corner_values * corner_choice[None, None], axis=4)
    arriving = jnp.concatenate(
        [strips.reshape(levels_here, tracers, tiles_here, 4 * EDGE), corner_picked], axis=3
    )
    returned = jnp.einsum(
        "dntr,rc->dntc", arriving, jnp.asarray(placing), precision=lax.Precision.HIGHEST
    )
    diffuse_here = diffusivity[None, None]
    return wet_mask[:, None] * ((1.0 - 5.0 * diffuse_here) * weighted + interior + returned)


PADDED = 1024
LANES = 128
GROUP = 32
PLANE = 8
MESH = pl.DeviceIdType.MESH


def boundary_cells():
    spots = []
    for j in range(EDGE):
        for side, cell in enumerate([j, (EDGE - 1) * EDGE + j, EDGE * j, EDGE * j + EDGE - 1]):
            spots.append((GROUP * side + j, cell))
    for corner, cell in enumerate([0, EDGE - 1, (EDGE - 1) * EDGE, EDGE * EDGE - 1]):
        spots.append((GROUP * corner + EDGE, cell))
    return spots


def boundary_gatherer():
    chosen = np.zeros((PADDED, LANES), np.float32)
    for lane, cell in boundary_cells():
        chosen[cell, lane] = 1.0
    return jnp.asarray(chosen, jnp.bfloat16)


def boundary_placer():
    placing = np.zeros((2 * LANES, PADDED), np.float32)
    for lane, cell in boundary_cells():
        placing[lane, cell] = 1.0
        placing[LANES + lane, cell] = 1.0
    return jnp.asarray(placing, jnp.bfloat16)


def halves(value):
    high = value.astype(jnp.bfloat16)
    return high, (value - high.astype(jnp.float32)).astype(jnp.bfloat16)


def widen(rows):
    return jnp.concatenate(
        [rows, jnp.zeros((rows.shape[0], PADDED - rows.shape[1]), rows.dtype)], axis=1
    )


def exchange_kernel(
    count,
    cot_hbm, cx_hbm, cy_hbm, dif_hbm, vd_hbm, lc_hbm, et_hbm, ec_hbm, ct_hbm, cc_hbm, sel_hbm, pla_hbm,
    out_ref,
    cot_ref, vdc_ref, cxc_ref, cyc_ref, dif_ref, lc_ref, vd_ref, cx_ref, cy_ref,
    lists_ref, code_ref, sel_ref, pla_ref,
    bcot_ref, bvd_ref, bflow_ref, strips_ref, factor_ref, partial_ref, base_ref,
    tables_ref, table_smem, near_ref, picked_ref, arriving_ref,
    in_sem, send_sem, recv_sem, tab_send, tab_recv, pick_send, pick_recv,
):
    levels = cot_ref.shape[0]
    quad = levels // 4
    chunk = levels // PLANE
    cells = cot_ref.shape[2]
    planes = count // PLANE
    me = lax.axis_index("tile")
    plane = me // PLANE
    here = lax.rem(me, PLANE)

    def at(step, turn):
        return PLANE * lax.rem(plane + step + planes, planes) + (here ^ turn)

    started = []

    def fetch(source, target):
        copy = pltpu.make_async_copy(source, target, in_sem.at[len(started)])
        copy.start()
        started.append(copy)
        return copy

    def fetch_quads(source, target):
        return [
            fetch(source.at[quad * j : quad * j + quad], target.at[:, 2 * j : 2 * j + 2])
            for j in range(4)
        ]

    def fetch_flat(source, target):
        return [fetch(source, target.at[2 * n : 2 * n + 2]) for n in range(4)]

    def fetch_wide(source, target):
        return [fetch(source, target.at[:, 2 * n : 2 * n + 2]) for n in range(4)]

    first = fetch_quads(vd_hbm, vdc_ref) + fetch_flat(lc_hbm, lc_ref)
    first += [fetch(sel_hbm, sel_ref)]
    second = [fetch(cot_hbm.at[:, n], cot_ref.at[:, 2 * n : 2 * n + 2]) for n in range(4)]
    third = fetch_quads(cx_hbm, cxc_ref) + fetch_quads(cy_hbm, cyc_ref)
    third += fetch_flat(dif_hbm, dif_ref) + [fetch(ec_hbm, code_ref)]
    lists = [
        fetch(source, lists_ref.at[i]) for i, source in enumerate([et_hbm, ec_hbm, ct_hbm, cc_hbm])
    ]

    barrier = pltpu.get_barrier_semaphore()
    steps = [(-1, turn) for turn in range(PLANE)] + [(1, turn) for turn in range(PLANE)]
    steps += [(0, turn) for turn in range(1, PLANE)]
    for step, turn in steps:
        pl.semaphore_signal(barrier, inc=1, device_id={"tile": at(step, turn)}, device_id_type=MESH)

    fourth = fetch_wide(vd_hbm, vd_ref)
    fifth = fetch_wide(cx_hbm, cx_ref) + fetch_wide(cy_hbm, cy_ref) + [fetch(pla_hbm, pla_ref)]

    lane = lax.broadcasted_iota(jnp.int32, (8, LANES), 1)
    row = lax.broadcasted_iota(jnp.int32, (8, LANES), 0)
    parity = row & 1
    group = lane // GROUP
    spot = lane & (GROUP - 1)
    on_side = spot < EDGE

    def gather(rows):
        high, low = halves(widen(rows))
        return jnp.dot(high, sel_ref[...], preferred_element_type=jnp.float32) + jnp.dot(
            low, sel_ref[...], preferred_element_type=jnp.float32
        )

    def spread_rows(values, j):
        return jnp.take_along_axis(values, 2 * j + parity, axis=0)

    for copy in first:
        copy.wait()
    bdepth = jnp.dot(
        widen(lc_ref[...].astype(jnp.float32)).astype(jnp.bfloat16),
        sel_ref[...],
        preferred_element_type=jnp.float32,
    )
    bvd_ref[...] = gather(vdc_ref[...].reshape(8 * quad, cells)).reshape(quad, 8, LANES)

    def bcoupling(k):
        if k == 0 or k == levels:
            return jnp.zeros((8, LANES), jnp.float32)
        return jnp.where(k < bdepth, spread_rows(bvd_ref[k % quad], k // quad), 0.0)

    for copy in second:
        copy.wait()
    bcot_ref[...] = gather(cot_ref[...].reshape(8 * levels, cells)).reshape(levels, 8, LANES)

    middle = levels // 2
    zero = jnp.zeros((8, LANES), jnp.float32)
    coupled = [bcoupling(k) for k in range(levels + 1)]
    link, value = [None] * levels, [None] * levels
    excess, part = zero + 1.0, zero
    low_excess, low_part = zero + 1.0, zero
    for k in range(middle):
        up, down = coupled[k], coupled[k + 1]
        source = bcot_ref[k] + up * part
        total = down + excess
        if k < middle - 1:
            inverse = 1.0 / total
            link[k] = down * inverse
            part = source * inverse
            value[k] = part
            excess = 1.0 + link[k] * excess
        else:
            top_source, top_excess, top_total = source, excess, total
        m = levels - 1 - k
        up, down = coupled[m], coupled[m + 1]
        source = bcot_ref[m] + down * low_part
        total = up + low_excess
        if k < middle - 1:
            inverse = 1.0 / total
            link[m] = up * inverse
            low_part = source * inverse
            value[m] = low_part
            low_excess = 1.0 + link[m] * low_excess
        else:
            low_source, low_excess_end, low_total = source, low_excess, total
    joint = coupled[middle]
    inverse = 1.0 / (joint * (top_excess + low_excess_end) + top_excess * low_excess_end)
    value[middle] = (low_source * top_total + joint * top_source) * inverse
    value[middle - 1] = (top_source * low_total + joint * low_source) * inverse
    for k in range(middle - 2, -1, -1):
        value[k] = value[k] + link[k] * value[k + 1]
    for k in range(middle + 1, levels):
        value[k] = value[k] + link[k] * value[k - 1]

    for copy in third:
        copy.wait()
    bdif = jnp.dot(halves(widen(dif_ref[...]))[0], sel_ref[...], preferred_element_type=jnp.float32)
    bdif = bdif + jnp.dot(
        halves(widen(dif_ref[...]))[1], sel_ref[...], preferred_element_type=jnp.float32
    )
    along = gather(cxc_ref[...].reshape(8 * quad, cells)).reshape(quad, 8, LANES)
    across = gather(cyc_ref[...].reshape(8 * quad, cells)).reshape(quad, 8, LANES)
    for g in range(quad):
        flow = 0.5 * jnp.where(group < 2, across[g], along[g])
        bflow_ref[g] = jnp.where(on_side, jnp.where((group & 1) == 0, flow, -flow), 0.0)
    code = jnp.zeros((8, LANES), jnp.int32)
    for i in range(2):
        for side in range(4):
            code = jnp.where((parity == i) & (group == side), code_ref[i, side], code)
    turned = jnp.where((code >= 4) & on_side, GROUP * group + (EDGE - 1) - spot, lane)
    quarter = 0.25 * bdif
    weight = jnp.where(on_side, bdif, quarter)
    for k in range(levels):
        u = jnp.where(k < bdepth, value[k], 0.0)
        diagonal = jnp.where(on_side, quarter * u, 0.0)
        beside = pltpu.roll(diagonal, 1, 1) + pltpu.roll(diagonal, LANES - 1, 1)
        halo = (weight + spread_rows(bflow_ref[k % quad], k // quad)) * u
        halo = halo + jnp.where(on_side, beside, 0.0)
        strips_ref[k] = jnp.take_along_axis(halo, turned, axis=1)

    for copy in lists:
        copy.wait()
    tile_index = lax.broadcasted_iota(jnp.int32, (2, 4), 0)
    side_index = lax.broadcasted_iota(jnp.int32, (2, 4), 1)
    tables_ref[here] = jnp.zeros((8, LANES), jnp.int32)
    for part_index in range(2):
        tile, kind = lists_ref[2 * part_index], lists_ref[2 * part_index + 1]
        device = tile >> 1
        step = device // PLANE - plane + 1
        step = jnp.where(step < 0, step + planes, step)
        step = jnp.where(step >= planes, step - planes, step)
        slot = PLANE * step + (device & (PLANE - 1))
        slot = jnp.where((tile < 0) | (step > 2), 3 * PLANE, slot)
        word = 2 * slot + ((tile & 1) ^ tile_index)
        word = 4 * word + ((side_index - (kind & 3)) & 3)
        tables_ref[here, 2 * part_index : 2 * part_index + 2, 0:4] = word

    pl.semaphore_wait(barrier, len(steps))
    copies = []
    for n, (step, turn) in enumerate(steps):
        slot = PLANE * (1 - step) + here
        copy = pltpu.make_async_remote_copy(
            src_ref=strips_ref.at[pl.ds(chunk * (here ^ turn), chunk)],
            dst_ref=near_ref.at[slot, 0],
            send_sem=send_sem.at[n],
            recv_sem=recv_sem.at[n],
            device_id={"tile": at(step, turn)},
            device_id_type=MESH,
        )
        copy.start()
        copies.append(copy)
    tells = []
    for turn in range(1, PLANE):
        copy = pltpu.make_async_remote_copy(
            src_ref=tables_ref.at[here],
            dst_ref=tables_ref.at[here],
            send_sem=tab_send.at[turn - 1],
            recv_sem=tab_recv.at[turn - 1],
            device_id={"tile": at(0, turn)},
            device_id_type=MESH,
        )
        copy.start()
        tells.append(copy)
    near_ref[PLANE + here, 0] = strips_ref[pl.ds(chunk * here, chunk)]
    near_ref[3 * PLANE] = jnp.zeros((2, chunk, 8, LANES), jnp.float32)

    for copy in fourth:
        copy.wait()
    depth = lc_ref[...]

    def advance(k, state):
        up, excess, part = state
        later = jnp.minimum(k + 1, levels - 1)
        down = jnp.where(k + 1 < depth, vd_ref[later], 0.0)
        down = jnp.where(k + 1 < levels, down, 0.0)
        inverse = 1.0 / (down + excess)
        factor = down * inverse
        part = (cot_ref[k] + up * part) * inverse
        factor_ref[k] = factor
        partial_ref[k] = part
        return down, 1.0 + factor * excess, part

    blank = jnp.zeros((8, cells), jnp.float32)
    lax.fori_loop(0, levels, advance, (blank, blank + 1.0, blank), unroll=2)

    for copy in fifth:
        copy.wait()
    wide_lane = lax.broadcasted_iota(jnp.int32, (8, PADDED), 1)
    wraps = PADDED - EDGE
    column = lax.rem(jnp.where(wide_lane >= wraps, wide_lane - wraps, wide_lane), EDGE)
    not_first = column != 0
    not_last = column != EDGE - 1
    diffuse = widen(dif_ref[...])
    quarter_wide = 0.25 * diffuse
    centre = 1.0 - 5.0 * diffuse
    wide_depth = widen(depth)

    def substitute_back(step, solved):
        k = levels - 1 - step
        solved = partial_ref[k] + factor_ref[k] * solved
        u = widen(jnp.where(k < depth, solved, 0.0))
        half_x = 0.5 * widen(cx_ref[k])
        half_y = 0.5 * widen(cy_ref[k])
        diagonal = quarter_wide * u
        both = pltpu.roll(diagonal, EDGE, 1) + pltpu.roll(diagonal, PADDED - EDGE, 1)
        west = both + (diffuse + half_x) * u
        east = both + (diffuse - half_x) * u
        total = pltpu.roll((diffuse + half_y) * u, PADDED - EDGE, 1)
        total = total + pltpu.roll((diffuse - half_y) * u, EDGE, 1)
        total = total + pltpu.roll(jnp.where(not_first, west, 0.0), PADDED - 1, 1)
        total = total + pltpu.roll(jnp.where(not_last, east, 0.0), 1, 1)
        base_ref[k] = jnp.where(k < wide_depth, centre * u + total, 0.0)
        return solved

    lax.fori_loop(0, levels, substitute_back, blank, unroll=2)

    for copy in tells:
        copy.wait_recv()
    to_smem = pltpu.make_async_copy(tables_ref, table_smem, in_sem.at[len(started)])
    to_smem.start()

    def swap_rows(slot):
        for t in range(chunk):
            near_ref[slot, 1, t] = jnp.take_along_axis(near_ref[slot, 0, t], row ^ 1, axis=0)

    swap_rows(PLANE + here)
    for n in reversed(range(len(steps))):
        step, turn = steps[n]
        copies[n].wait_recv()
        swap_rows(PLANE * (1 + step) + (here ^ turn) if step == 0 else PLANE * (1 - step) + (here ^ turn))
    to_smem.wait()

    flat = near_ref
    picks = []
    for turn in list(range(1, PLANE)) + [0]:
        total = jnp.zeros((chunk, 8, LANES), jnp.float32)
        for kind in range(2):
            wanted = on_side if kind == 0 else spot == EDGE
            for i in range(2):
                for side in range(4):
                    word = table_smem[here ^ turn, 2 * kind + i, side]
                    values = flat[word >> 3, (word >> 2) & 1]
                    values = pltpu.roll(values, GROUP * (word & 3), 2)
                    chosen = wanted & (group == side) & (parity == i)
                    total = jnp.where(chosen[None], values, total)
        if turn == 0:
            arriving_ref[pl.ds(chunk * here, chunk)] = total
            continue
        picked_ref[turn - 1] = total
        copy = pltpu.make_async_remote_copy(
            src_ref=picked_ref.at[turn - 1],
            dst_ref=arriving_ref.at[pl.ds(chunk * here, chunk)],
            send_sem=pick_send.at[turn - 1],
            recv_sem=pick_recv.at[turn - 1],
            device_id={"tile": at(0, turn)},
            device_id_type=MESH,
        )
        copy.start()
        picks.append(copy)

    for turn in range(PLANE):
        if turn:
            picks[turn - 1].wait_recv()
        start = chunk * (here ^ turn)
        rows = [
            jnp.where(start + t < bdepth, arriving_ref[start + t], 0.0) for t in range(chunk)
        ]
        high, low = halves(jnp.concatenate(rows, axis=0))
        returned = jnp.dot(
            jnp.concatenate([high, low], axis=1), pla_ref[...], preferred_element_type=jnp.float32
        )
        for t in range(chunk):
            result = base_ref[start + t] + returned[8 * t : 8 * t + 8]
            out_ref[start + t] = result[:, :cells]
    for copy in copies + tells + picks:
        copy.wait_send()


def store_kernel(held_ref, out_hbm, sems):
    copies = [
        pltpu.make_async_copy(held_ref.at[:, 2 * n : 2 * n + 2], out_hbm.at[:, n], sems.at[n])
        for n in range(4)
    ]
    for copy in copies:
        copy.start()
    for copy in copies:
        copy.wait()


def shards_fast(
    cotangent,
    courant_x,
    courant_y,
    diffusivity,
    vert_diff,
    level_count,
    edge_tile,
    edge_code,
    corner_tile,
    corner_code,
):
    levels, tracers, tiles_here, cells = cotangent.shape
    count = lax.axis_size("tile")
    vmem = pl.BlockSpec(memory_space=pltpu.VMEM)
    hbm = pl.BlockSpec(memory_space=pltpu.HBM)
    chunk = levels // PLANE
    f32 = jnp.float32
    held = pl.pallas_call(
        functools.partial(exchange_kernel, count),
        name="exchange",
        out_shape=pltpu.VMEM((levels, 8, cells), f32),
        in_specs=[hbm] * 12,
        out_specs=vmem,
        scratch_shapes=[
            pltpu.VMEM((levels, 8, cells), f32),
            pltpu.VMEM((levels // 4, 8, cells), f32),
            pltpu.VMEM((levels // 4, 8, cells), f32),
            pltpu.VMEM((levels // 4, 8, cells), f32),
            pltpu.VMEM((8, cells), f32),
            pltpu.VMEM((8, cells), jnp.int32),
            pltpu.VMEM((levels, 8, cells), f32),
            pltpu.VMEM((levels, 8, cells), f32),
            pltpu.VMEM((levels, 8, cells), f32),
            pltpu.VMEM((4, 2, 4), jnp.int32),
            pltpu.SMEM((2, 4), jnp.int32),
            pltpu.VMEM((PADDED, LANES), jnp.bfloat16),
            pltpu.VMEM((2 * LANES, PADDED), jnp.bfloat16),
            pltpu.VMEM((levels, 8, LANES), f32),
            pltpu.VMEM((levels // 4, 8, LANES), f32),
            pltpu.VMEM((levels // 4, 8, LANES), f32),
            pltpu.VMEM((levels, 8, LANES), f32),
            pltpu.VMEM((levels, 8, cells), f32),
            pltpu.VMEM((levels, 8, cells), f32),
            pltpu.VMEM((levels, 8, PADDED), f32),
            pltpu.VMEM((PLANE, 8, LANES), jnp.int32),
            pltpu.SMEM((PLANE, 8, LANES), jnp.int32),
            pltpu.VMEM((3 * PLANE + 1, 2, chunk, 8, LANES), f32),
            pltpu.VMEM((PLANE - 1, chunk, 8, LANES), f32),
            pltpu.VMEM((levels, 8, LANES), f32),
            pltpu.SemaphoreType.DMA((64,)),
            pltpu.SemaphoreType.DMA((3 * PLANE - 1,)),
            pltpu.SemaphoreType.DMA((3 * PLANE - 1,)),
            pltpu.SemaphoreType.DMA((PLANE - 1,)),
            pltpu.SemaphoreType.DMA((PLANE - 1,)),
            pltpu.SemaphoreType.DMA((PLANE - 1,)),
            pltpu.SemaphoreType.DMA((PLANE - 1,)),
        ],
        compiler_params=pltpu.CompilerParams(
            collective_id=0, has_side_effects=True, vmem_limit_bytes=62 << 20
        ),
    )(
        cotangent, courant_x, courant_y, diffusivity, vert_diff, level_count,
        edge_tile, edge_code, corner_tile, corner_code, boundary_gatherer(), boundary_placer(),
    )
    return pl.pallas_call(
        store_kernel,
        name="store",
        out_shape=jax.ShapeDtypeStruct(cotangent.shape, f32),
        in_specs=[vmem],
        out_specs=hbm,
        scratch_shapes=[pltpu.SemaphoreType.DMA((4,))],
        compiler_params=pltpu.CompilerParams(vmem_limit_bytes=8 << 20),
    )(held)


def solution(mesh):
    placed = (
        P("lev", None, "tile", None),
        P("lev", "tile", None),
        P("lev", "tile", None),
        P("tile", None),
        P("lev", "tile", None),
        P("tile", None),
        P("tile", None),
        P("tile", None),
        P("tile", None),
        P("tile", None),
    )
    fast = mesh.shape["lev"] == 1 and mesh.shape["tile"] % PLANE == 0 and mesh.shape["tile"] > 2 * BAND
    return jax.shard_map(
        shards_fast if fast else shards, mesh=mesh, in_specs=placed, out_specs=P("lev", None, "tile", None), check_vma=False
    )
```

```python
import functools

import jax
import jax.numpy as jnp
import numpy as np
from jax import lax
from jax.experimental import pallas as pl
from jax.experimental.pallas import tpu as pltpu
from jax.sharding import PartitionSpec as P

EDGE = 30
BAND = 8


stencil_offsets = [(0, -1), (0, 1), (-1, 0), (1, 0), (-1, -1), (-1, 1), (1, -1), (1, 1)]


def from_behind(value, axis, steps):
    count = lax.axis_size(axis)
    initial, last = (max(0, -steps), min(count, count - steps))
    return lax.ppermute(value, axis, [(source, source + steps) for source in range(initial, last)])


def shifted_2(value, axis, by):
    devices = lax.axis_size(axis)
    return lax.ppermute(value, axis, [(i, (i + by) % devices) for i in range(devices)])


def stencil_weights(diffuse, flow_x, flow_y):
    return [
        diffuse + 0.5 * flow_x,
        diffuse - 0.5 * flow_x,
        diffuse + 0.5 * flow_y,
        diffuse - 0.5 * flow_y,
        0.25 * diffuse,
        0.25 * diffuse,
        0.25 * diffuse,
        0.25 * diffuse,
    ]


def eliminate(right_side, coupling_up, coupling_down, initial):

    def advance(state, inputs):
        factor, partial_value = state
        source, upper_term, lower_term = inputs
        divisor = 1.0 + upper_term + lower_term + upper_term * factor
        factor_new = -lower_term / divisor
        partial_new = (source + upper_term * partial_value) / divisor
        return ((factor_new, partial_new), (factor_new, partial_new))

    final_state, outputs = lax.scan(advance, initial, (right_side, coupling_up, coupling_down))
    return outputs


def substitute(factors, partials, below_field):

    def backward(state, inputs):
        factor, partial_value = inputs
        column_value = partial_value - factor * state
        return (column_value, column_value)

    final_state, fields = lax.scan(backward, below_field, (factors, partials), reverse=True)
    return fields


def placing_table():
    cells = []
    for border in range(4):
        for position in range(EDGE):
            cells.append(
                [position, (EDGE - 1) * EDGE + position, position * EDGE, position * EDGE + EDGE - 1][border]
            )
    cells += [0, EDGE - 1, (EDGE - 1) * EDGE, EDGE * EDGE - 1]
    placing = np.zeros((len(cells), EDGE * EDGE), np.float32)
    placing[np.arange(len(cells)), np.array(cells)] = 1.0
    return placing


def embed(field):
    leading = field.shape[:-1]
    square = field.reshape(leading + (EDGE, EDGE))
    padded = jnp.pad(square, [(0, 0)] * len(leading) + [(1, 1), (1, 1)])
    return padded.reshape(leading + ((EDGE + 2) * (EDGE + 2),))


def shards(
    cotangent,
    courant_x,
    courant_y,
    diffusivity,
    vert_diff,
    level_count,
    edge_tile,
    edge_code,
    corner_tile,
    corner_code,
):
    levels_here = cotangent.shape[0]
    tracers = cotangent.shape[1]
    tiles_here = cotangent.shape[2]
    cells = cotangent.shape[3]
    padded_edge = EDGE + 2
    cycle_size = 4 * EDGE + 4
    lev_count = lax.axis_size("lev")
    depth_index = (
        lax.axis_index("lev") * levels_here
        + jnp.arange(levels_here, dtype=jnp.int32)[:, None, None]
    )
    wet_mask = (depth_index < level_count[None]).astype(jnp.float32)
    coupling = jnp.where(depth_index == 0, jnp.float32(0.0), vert_diff * wet_mask)
    deeper = from_behind(coupling[0], "lev", -1)
    coupling_down = jnp.concatenate([coupling[1:], deeper[None]], axis=0)[:, None]
    coupling_up = coupling[:, None]
    initial = (
        jnp.zeros((1, tiles_here, cells), jnp.float32),
        jnp.zeros((tracers, tiles_here, cells), jnp.float32),
    )
    for sweep_index in range(lev_count - 1):
        factors, partials = eliminate(cotangent, coupling_up, coupling_down, initial)
        initial = from_behind((factors[-1], partials[-1]), "lev", 1)
    factors, partials = eliminate(cotangent, coupling_up, coupling_down, initial)
    below_field = jnp.zeros((tracers, tiles_here, cells), jnp.float32)
    for sweep_index in range(lev_count - 1):
        fields = substitute(factors, partials, below_field)
        below_field = from_behind(fields[0], "lev", -1)
    solved = substitute(factors, partials, below_field)
    weighted = solved * wet_mask[:, None]
    weighted_ext = embed(weighted)
    diffuse_ext = embed(diffusivity)[None, None]
    flow_x_ext = embed(courant_x)[:, None]
    flow_y_ext = embed(courant_y)[:, None]
    weights = stencil_weights(diffuse_ext, flow_x_ext, flow_y_ext)
    leading = weighted_ext.shape[:-1]
    spread = jnp.zeros_like(weighted_ext)
    for (shift_row, shift_col), weight in zip(stencil_offsets, weights):
        contribution = weight * weighted_ext
        offset = shift_row * padded_edge + shift_col
        if offset > 0:
            shifted = jnp.concatenate(
                [jnp.zeros(leading + (offset,), jnp.float32), contribution[..., :-offset]], axis=-1
            )
        else:
            shifted = jnp.concatenate(
                [contribution[..., -offset:], jnp.zeros(leading + (-offset,), jnp.float32)], axis=-1
            )
        spread = spread + shifted
    placing = placing_table()
    framed = spread.reshape(leading + (padded_edge, padded_edge))
    outgoing = jnp.concatenate(
        [
            framed[..., 0, 1:-1],
            framed[..., -1, 1:-1],
            framed[..., 1:-1, 0],
            framed[..., 1:-1, -1],
            framed[..., 0, :1],
            framed[..., 0, -1:],
            framed[..., -1, :1],
            framed[..., -1, -1:],
        ],
        axis=-1,
    )
    interior = spread.reshape(leading + (padded_edge, padded_edge))[..., 1:-1, 1:-1].reshape(
        solved.shape
    )
    partners = jnp.concatenate([edge_tile, corner_tile], axis=1)

    def collect(gathered_sum, portion, first_tile):
        tile_span = portion.shape[2]
        onehot = (
            partners[:, :, None]
            == first_tile + jnp.arange(tile_span, dtype=jnp.int32)[None, None, :]
        ).astype(jnp.float32)
        return gathered_sum + jnp.einsum(
            "tkw,dnwr->dntkr", onehot, portion, precision=lax.Precision.HIGHEST
        )

    tile_count = lax.axis_size("tile")
    own_index = lax.axis_index("tile")
    reach = (2 * BAND + tiles_here - 1) // tiles_here
    fetched = collect(
        jnp.zeros((levels_here, tracers, tiles_here, 8, cycle_size), jnp.float32),
        outgoing,
        own_index * tiles_here,
    )
    for distance in range(-reach, reach + 1):
        if distance != 0:
            portion = shifted_2(outgoing, "tile", distance)
            source = (own_index - distance) % tile_count
            fetched = collect(fetched, portion, source * tiles_here)
    side_values = fetched[:, :, :, :4, : 4 * EDGE].reshape(
        levels_here, tracers, tiles_here, 4, 4, EDGE
    )
    side_choice = (
        (edge_code % 4)[:, :, None] == jnp.arange(4, dtype=jnp.int32)[None, None, :]
    ).astype(jnp.float32)
    strips = jnp.sum(side_values * side_choice[None, None, :, :, :, None], axis=4)
    strips = jnp.where((edge_code >= 4)[None, None, :, :, None], strips[..., ::-1], strips)
    corner_values = fetched[:, :, :, 4:, 4 * EDGE :]
    corner_choice = (
        corner_code[:, :, None] == jnp.arange(4, dtype=jnp.int32)[None, None, :]
    ).astype(jnp.float32)
    corner_picked = jnp.sum(corner_values * corner_choice[None, None], axis=4)
    arriving = jnp.concatenate(
        [strips.reshape(levels_here, tracers, tiles_here, 4 * EDGE), corner_picked], axis=3
    )
    returned = jnp.einsum(
        "dntr,rc->dntc", arriving, jnp.asarray(placing), precision=lax.Precision.HIGHEST
    )
    diffuse_here = diffusivity[None, None]
    return wet_mask[:, None] * ((1.0 - 5.0 * diffuse_here) * weighted + interior + returned)


PADDED = 1024
LANES = 128
GROUP = 32
PLANE = 8
MESH = pl.DeviceIdType.MESH
PICK_SEMS = {1: 2, 3: 3, 2: 3, 5: 3, 4: 3, 7: 4, 6: 4}
PICK_WAITS = {1: 1, 3: 4, 7: 2}


def boundary_cells():
    spots = []
    for j in range(EDGE):
        for side, cell in enumerate([j, (EDGE - 1) * EDGE + j, EDGE * j, EDGE * j + EDGE - 1]):
            spots.append((GROUP * side + j, cell))
    for corner, cell in enumerate([0, EDGE - 1, (EDGE - 1) * EDGE, EDGE * EDGE - 1]):
        spots.append((GROUP * corner + EDGE, cell))
    return spots


def boundary_gatherer():
    chosen = np.zeros((PADDED, LANES), np.float32)
    for lane, cell in boundary_cells():
        chosen[cell, lane] = 1.0
    return jnp.asarray(chosen, jnp.bfloat16)


def boundary_placer():
    placing = np.zeros((2 * LANES, PADDED), np.float32)
    for lane, cell in boundary_cells():
        placing[lane, cell] = 1.0
        placing[LANES + lane, cell] = 1.0
    return jnp.asarray(placing, jnp.bfloat16)


def halves(value):
    high = value.astype(jnp.bfloat16)
    return high, (value - high.astype(jnp.float32)).astype(jnp.bfloat16)


def widen(rows):
    return jnp.concatenate(
        [rows, jnp.zeros((rows.shape[0], PADDED - rows.shape[1]), rows.dtype)], axis=1
    )


def exchange_kernel(
    count,
    cot_hbm, cx_hbm, cy_hbm, dif_hbm, vd_hbm, lc_hbm, et_hbm, ec_hbm, ct_hbm, cc_hbm, sel_hbm, pla_hbm,
    out_ref,
    cot_ref, vdc_ref, cxc_ref, cyc_ref, dif_ref, lc_ref, vd_ref, cx_ref, cy_ref,
    lists_ref, code_ref, sel_ref, pla_ref,
    bcot_ref, bvd_ref, bflow_ref, strips_ref, factor_ref, partial_ref, base_ref,
    tables_ref, table_smem, near_ref, picked_ref, arriving_ref,
    in_sem, send_sem, recv_sem,
):
    levels = cot_ref.shape[0]
    quad = levels // 4
    chunk = levels // PLANE
    cells = cot_ref.shape[2]
    planes = count // PLANE
    me = lax.axis_index("tile")
    plane = me // PLANE
    here = lax.rem(me, PLANE)

    def at(step, turn):
        return PLANE * lax.rem(plane + step + planes, planes) + (here ^ turn)

    low_end, high_end = (planes - plane) // planes, (plane + 1) // planes
    inner = 1 - low_end - high_end
    leap = low_end + high_end - inner
    order = [leap, 0, -leap]
    turns = [6, 7, 4, 5, 2, 3, 1, 0]

    barrier = pltpu.get_barrier_semaphore()
    peers = [(step, turn) for step in order for turn in turns if turn] + [(leap, 0), (-leap, 0)]
    for step, turn in peers:
        pl.semaphore_signal(barrier, inc=1, device_id={"tile": at(step, turn)}, device_id_type=MESH)

    used = []

    def fetch(pairs, whole):
        sem = in_sem.at[len(used)]
        used.append(whole)
        for source, target in pairs:
            pltpu.make_async_copy(source, target, sem).start()
        return pltpu.make_async_copy(whole, whole, sem)

    def fetch_quads(source, target):
        return fetch(
            [
                (source.at[quad * j : quad * j + quad], target.at[:, 2 * j : 2 * j + 2])
                for j in range(4)
            ],
            target,
        )

    def fetch_flat(source, target):
        return fetch([(source, target.at[2 * n : 2 * n + 2]) for n in range(4)], target)

    def fetch_wide(source, target):
        return fetch([(source, target.at[:, 2 * n : 2 * n + 2]) for n in range(4)], target)

    first = [fetch_quads(vd_hbm, vdc_ref), fetch_flat(lc_hbm, lc_ref), fetch([(sel_hbm, sel_ref)], sel_ref)]
    second = [
        fetch([(cot_hbm.at[:, n], cot_ref.at[:, 2 * n : 2 * n + 2]) for n in range(4)], cot_ref)
    ]
    third = [fetch_quads(cx_hbm, cxc_ref), fetch_quads(cy_hbm, cyc_ref)]
    third += [fetch_flat(dif_hbm, dif_ref), fetch([(ec_hbm, code_ref)], code_ref)]
    lists = fetch(
        [(source, lists_ref.at[i]) for i, source in enumerate([et_hbm, ec_hbm, ct_hbm, cc_hbm])],
        lists_ref,
    )
    fourth = [fetch_wide(vd_hbm, vd_ref)]
    fifth = [fetch_wide(cx_hbm, cx_ref), fetch_wide(cy_hbm, cy_ref), fetch([(pla_hbm, pla_ref)], pla_ref)]

    lane = lax.broadcasted_iota(jnp.int32, (8, LANES), 1)
    row = lax.broadcasted_iota(jnp.int32, (8, LANES), 0)
    parity = row & 1
    group = lane // GROUP
    spot = lane & (GROUP - 1)
    on_side = spot < EDGE

    def gather(rows):
        high, low = halves(widen(rows))
        return jnp.dot(high, sel_ref[...], preferred_element_type=jnp.float32) + jnp.dot(
            low, sel_ref[...], preferred_element_type=jnp.float32
        )

    def spread_rows(values, j):
        return jnp.take_along_axis(values, 2 * j + parity, axis=0)

    for copy in first:
        copy.wait()
    bdepth = jnp.dot(
        widen(lc_ref[...].astype(jnp.float32)).astype(jnp.bfloat16),
        sel_ref[...],
        preferred_element_type=jnp.float32,
    )
    bvd_ref[...] = gather(vdc_ref[...].reshape(8 * quad, cells)).reshape(quad, 8, LANES)

    def bcoupling(k):
        if k == 0 or k == levels:
            return jnp.zeros((8, LANES), jnp.float32)
        return jnp.where(k < bdepth, spread_rows(bvd_ref[k % quad], k // quad), 0.0)

    for copy in second:
        copy.wait()
    bcot_ref[...] = gather(cot_ref[...].reshape(8 * levels, cells)).reshape(levels, 8, LANES)

    middle = levels // 2
    zero = jnp.zeros((8, LANES), jnp.float32)
    coupled = [bcoupling(k) for k in range(levels + 1)]
    link, value = [None] * levels, [None] * levels
    excess, part = zero + 1.0, zero
    low_excess, low_part = zero + 1.0, zero
    for k in range(middle):
        up, down = coupled[k], coupled[k + 1]
        source = bcot_ref[k] + up * part
        total = down + excess
        if k < middle - 1:
            inverse = 1.0 / total
            link[k] = down * inverse
            part = source * inverse
            value[k] = part
            excess = 1.0 + link[k] * excess
        else:
            top_source, top_excess, top_total = source, excess, total
        m = levels - 1 - k
        up, down = coupled[m], coupled[m + 1]
        source = bcot_ref[m] + down * low_part
        total = up + low_excess
        if k < middle - 1:
            inverse = 1.0 / total
            link[m] = up * inverse
            low_part = source * inverse
            value[m] = low_part
            low_excess = 1.0 + link[m] * low_excess
        else:
            low_source, low_excess_end, low_total = source, low_excess, total
    joint = coupled[middle]
    inverse = 1.0 / (joint * (top_excess + low_excess_end) + top_excess * low_excess_end)
    value[middle] = (low_source * top_total + joint * top_source) * inverse
    value[middle - 1] = (top_source * low_total + joint * low_source) * inverse
    for k in range(middle - 2, -1, -1):
        value[k] = value[k] + link[k] * value[k + 1]
    for k in range(middle + 1, levels):
        value[k] = value[k] + link[k] * value[k - 1]

    for copy in third:
        copy.wait()
    bdif = jnp.dot(halves(widen(dif_ref[...]))[0], sel_ref[...], preferred_element_type=jnp.float32)
    bdif = bdif + jnp.dot(
        halves(widen(dif_ref[...]))[1], sel_ref[...], preferred_element_type=jnp.float32
    )
    along = gather(cxc_ref[...].reshape(8 * quad, cells)).reshape(quad, 8, LANES)
    across = gather(cyc_ref[...].reshape(8 * quad, cells)).reshape(quad, 8, LANES)
    for g in range(quad):
        flow = 0.5 * jnp.where(group < 2, across[g], along[g])
        bflow_ref[g] = jnp.where(on_side, jnp.where((group & 1) == 0, flow, -flow), 0.0)
    code = jnp.zeros((8, LANES), jnp.int32)
    for i in range(2):
        for side in range(4):
            code = jnp.where((parity == i) & (group == side), code_ref[i, side], code)
    turned = jnp.where((code >= 4) & on_side, GROUP * group + (EDGE - 1) - spot, lane)
    quarter = 0.25 * bdif
    weight = jnp.where(on_side, bdif, quarter)
    for k in range(levels):
        u = jnp.where(k < bdepth, value[k], 0.0)
        diagonal = jnp.where(on_side, quarter * u, 0.0)
        beside = pltpu.roll(diagonal, 1, 1) + pltpu.roll(diagonal, LANES - 1, 1)
        halo = (weight + spread_rows(bflow_ref[k % quad], k // quad)) * u
        halo = halo + jnp.where(on_side, beside, 0.0)
        strips_ref[k] = jnp.take_along_axis(halo, turned, axis=1)

    lists.wait()
    tile_index = lax.broadcasted_iota(jnp.int32, (2, 4), 0)
    side_index = lax.broadcasted_iota(jnp.int32, (2, 4), 1)
    tables_ref[here] = jnp.zeros((8, LANES), jnp.int32)
    for part_index in range(2):
        tile, kind = lists_ref[2 * part_index], lists_ref[2 * part_index + 1]
        device = tile >> 1
        step = device // PLANE - plane + 1
        step = jnp.where(step < 0, step + planes, step)
        step = jnp.where(step >= planes, step - planes, step)
        slot = PLANE * step + (device & (PLANE - 1))
        slot = jnp.where((tile < 0) | (step > 2), 3 * PLANE, slot)
        word = 2 * slot + ((tile & 1) ^ tile_index)
        word = 4 * word + ((side_index - (kind & 3)) & 3)
        tables_ref[here, 2 * part_index : 2 * part_index + 2, 0:4] = word

    pl.semaphore_wait(barrier, len(peers))

    def send(step, turn):
        pltpu.make_async_remote_copy(
            src_ref=strips_ref.at[pl.ds(chunk * (here ^ turn), chunk)],
            dst_ref=near_ref.at[0, PLANE * (1 - step) + here],
            send_sem=send_sem.at[0],
            recv_sem=recv_sem.at[0],
            device_id={"tile": at(step, turn)},
            device_id_type=MESH,
        ).start()

    def whole(source, target, mark):
        return pltpu.make_async_remote_copy(
            src_ref=source,
            dst_ref=target,
            send_sem=send_sem.at[mark],
            recv_sem=recv_sem.at[mark],
            device_id={"tile": at(0, 1)},
            device_id_type=MESH,
        )

    for turn in turns:
        send(leap, turn)
    for turn in turns[:-1]:
        send(0, turn)
    for turn in turns:
        send(-leap, turn)
    for turn in turns[:-1]:
        pltpu.make_async_remote_copy(
            src_ref=tables_ref.at[here],
            dst_ref=tables_ref.at[here],
            send_sem=send_sem.at[1],
            recv_sem=recv_sem.at[1],
            device_id={"tile": at(0, turn)},
            device_id_type=MESH,
        ).start()
    near_ref[0, PLANE + here] = strips_ref[pl.ds(chunk * here, chunk)]
    near_ref[:, 3 * PLANE] = jnp.zeros((2, chunk, 8, LANES), jnp.float32)

    for copy in fourth:
        copy.wait()
    depth = lc_ref[...]

    def advance(k, state):
        up, excess, part = state
        later = jnp.minimum(k + 1, levels - 1)
        down = jnp.where(k + 1 < depth, vd_ref[later], 0.0)
        down = jnp.where(k + 1 < levels, down, 0.0)
        inverse = 1.0 / (down + excess)
        factor = down * inverse
        part = (cot_ref[k] + up * part) * inverse
        factor_ref[k] = factor
        partial_ref[k] = part
        return down, 1.0 + factor * excess, part

    blank = jnp.zeros((8, cells), jnp.float32)
    lax.fori_loop(0, levels, advance, (blank, blank + 1.0, blank), unroll=2)

    for copy in fifth:
        copy.wait()
    wide_lane = lax.broadcasted_iota(jnp.int32, (8, PADDED), 1)
    wraps = PADDED - EDGE
    column = lax.rem(jnp.where(wide_lane >= wraps, wide_lane - wraps, wide_lane), EDGE)
    not_first = column != 0
    not_last = column != EDGE - 1
    diffuse = widen(dif_ref[...])
    quarter_wide = 0.25 * diffuse
    centre = 1.0 - 5.0 * diffuse
    wide_depth = widen(depth)

    def substitute_back(step, solved):
        k = levels - 1 - step
        solved = partial_ref[k] + factor_ref[k] * solved
        u = widen(jnp.where(k < depth, solved, 0.0))
        half_x = 0.5 * widen(cx_ref[k])
        half_y = 0.5 * widen(cy_ref[k])
        diagonal = quarter_wide * u
        both = pltpu.roll(diagonal, EDGE, 1) + pltpu.roll(diagonal, PADDED - EDGE, 1)
        west = both + (diffuse + half_x) * u
        east = both + (diffuse - half_x) * u
        total = pltpu.roll((diffuse + half_y) * u, PADDED - EDGE, 1)
        total = total + pltpu.roll((diffuse - half_y) * u, EDGE, 1)
        total = total + pltpu.roll(jnp.where(not_first, west, 0.0), PADDED - 1, 1)
        total = total + pltpu.roll(jnp.where(not_last, east, 0.0), 1, 1)
        base_ref[k] = jnp.where(k < wide_depth, centre * u + total, 0.0)
        return solved

    lax.fori_loop(0, levels, substitute_back, blank, unroll=2)

    others = pl.ds(0, PLANE - 1)
    told = whole(tables_ref.at[others], tables_ref.at[others], 1)
    told.wait_recv()
    to_smem = pltpu.make_async_copy(tables_ref, table_smem, in_sem.at[len(used)])
    to_smem.start()

    every = near_ref.at[0, pl.ds(0, 3 * PLANE - 1)]
    gathered = whole(every, every, 0)
    gathered.wait_recv()
    for slot in range(3 * PLANE):
        for t in range(chunk):
            near_ref[1, slot, t] = jnp.take_along_axis(near_ref[0, slot, t], row ^ 1, axis=0)
    to_smem.wait()

    for turn in turns:
        total = jnp.zeros((chunk, 8, LANES), jnp.float32)
        for kind in range(2):
            wanted = on_side if kind == 0 else spot == EDGE
            for i in range(2):
                for side in range(4):
                    word = table_smem[here ^ turn, 2 * kind + i, side]
                    values = near_ref[(word >> 2) & 1, word >> 3]
                    values = pltpu.roll(values, GROUP * (word & 3), 2)
                    chosen = wanted & (group == side) & (parity == i)
                    total = jnp.where(chosen[None], values, total)
        if turn == 0:
            arriving_ref[pl.ds(chunk * here, chunk)] = total
            continue
        picked_ref[turn - 1] = total
        pltpu.make_async_remote_copy(
            src_ref=picked_ref.at[turn - 1],
            dst_ref=arriving_ref.at[pl.ds(chunk * here, chunk)],
            send_sem=send_sem.at[2],
            recv_sem=recv_sem.at[PICK_SEMS[turn]],
            device_id={"tile": at(0, turn)},
            device_id_type=MESH,
        ).start()

    for turn in reversed(turns):
        if turn in PICK_WAITS:
            some = arriving_ref.at[pl.ds(0, chunk * PICK_WAITS[turn])]
            whole(some, some, PICK_SEMS[turn]).wait_recv()
        start = chunk * (here ^ turn)
        rows = [
            jnp.where(start + t < bdepth, arriving_ref[start + t], 0.0) for t in range(chunk)
        ]
        high, low = halves(jnp.concatenate(rows, axis=0))
        returned = jnp.dot(
            jnp.concatenate([high, low], axis=1), pla_ref[...], preferred_element_type=jnp.float32
        )
        for t in range(chunk):
            result = base_ref[start + t] + returned[8 * t : 8 * t + 8]
            out_ref[start + t] = result[:, :cells]
    gathered.wait_send()
    told.wait_send()
    whole(picked_ref, picked_ref, 2).wait_send()


def store_kernel(held_ref, out_hbm, sem):
    for n in range(4):
        pltpu.make_async_copy(held_ref.at[:, 2 * n : 2 * n + 2], out_hbm.at[:, n], sem).start()
    pltpu.make_async_copy(out_hbm, out_hbm, sem).wait()


def shards_fast(
    cotangent,
    courant_x,
    courant_y,
    diffusivity,
    vert_diff,
    level_count,
    edge_tile,
    edge_code,
    corner_tile,
    corner_code,
):
    levels, tracers, tiles_here, cells = cotangent.shape
    count = lax.axis_size("tile")
    vmem = pl.BlockSpec(memory_space=pltpu.VMEM)
    hbm = pl.BlockSpec(memory_space=pltpu.HBM)
    chunk = levels // PLANE
    f32 = jnp.float32
    held = pl.pallas_call(
        functools.partial(exchange_kernel, count),
        name="exchange",
        out_shape=pltpu.VMEM((levels, 8, cells), f32),
        in_specs=[hbm] * 12,
        out_specs=vmem,
        scratch_shapes=[
            pltpu.VMEM((levels, 8, cells), f32),
            pltpu.VMEM((levels // 4, 8, cells), f32),
            pltpu.VMEM((levels // 4, 8, cells), f32),
            pltpu.VMEM((levels // 4, 8, cells), f32),
            pltpu.VMEM((8, cells), f32),
            pltpu.VMEM((8, cells), jnp.int32),
            pltpu.VMEM((levels, 8, cells), f32),
            pltpu.VMEM((levels, 8, cells), f32),
            pltpu.VMEM((levels, 8, cells), f32),
            pltpu.VMEM((4, 2, 4), jnp.int32),
            pltpu.SMEM((2, 4), jnp.int32),
            pltpu.VMEM((PADDED, LANES), jnp.bfloat16),
            pltpu.VMEM((2 * LANES, PADDED), jnp.bfloat16),
            pltpu.VMEM((levels, 8, LANES), f32),
            pltpu.VMEM((levels // 4, 8, LANES), f32),
            pltpu.VMEM((levels // 4, 8, LANES), f32),
            pltpu.VMEM((levels, 8, LANES), f32),
            pltpu.VMEM((levels, 8, cells), f32),
            pltpu.VMEM((levels, 8, cells), f32),
            pltpu.VMEM((levels, 8, PADDED), f32),
            pltpu.VMEM((PLANE, 8, LANES), jnp.int32),
            pltpu.SMEM((PLANE, 8, LANES), jnp.int32),
            pltpu.VMEM((2, 3 * PLANE + 1, chunk, 8, LANES), f32),
            pltpu.VMEM((PLANE - 1, chunk, 8, LANES), f32),
            pltpu.VMEM((levels, 8, LANES), f32),
            pltpu.SemaphoreType.DMA((14,)),
            pltpu.SemaphoreType.DMA((3,)),
            pltpu.SemaphoreType.DMA((5,)),
        ],
        compiler_params=pltpu.CompilerParams(
            collective_id=0, has_side_effects=True, vmem_limit_bytes=62 << 20
        ),
    )(
        cotangent, courant_x, courant_y, diffusivity, vert_diff, level_count,
        edge_tile, edge_code, corner_tile, corner_code, boundary_gatherer(), boundary_placer(),
    )
    return pl.pallas_call(
        store_kernel,
        name="store",
        out_shape=jax.ShapeDtypeStruct(cotangent.shape, f32),
        in_specs=[vmem],
        out_specs=hbm,
        scratch_shapes=[pltpu.SemaphoreType.DMA],
        compiler_params=pltpu.CompilerParams(vmem_limit_bytes=8 << 20),
    )(held)


def solution(mesh):
    placed = (
        P("lev", None, "tile", None),
        P("lev", "tile", None),
        P("lev", "tile", None),
        P("tile", None),
        P("lev", "tile", None),
        P("tile", None),
        P("tile", None),
        P("tile", None),
        P("tile", None),
        P("tile", None),
    )
    fast = mesh.shape["lev"] == 1 and mesh.shape["tile"] % PLANE == 0 and mesh.shape["tile"] > 2 * BAND
    return jax.shard_map(
        shards_fast if fast else shards, mesh=mesh, in_specs=placed, out_specs=P("lev", None, "tile", None), check_vma=False
    )
```

```python
import functools

import jax
import jax.numpy as jnp
import numpy as np
from jax import lax
from jax.experimental import pallas as pl
from jax.experimental.pallas import tpu as pltpu
from jax.sharding import PartitionSpec as P

EDGE = 30
BAND = 8


stencil_offsets = [(0, -1), (0, 1), (-1, 0), (1, 0), (-1, -1), (-1, 1), (1, -1), (1, 1)]


def from_behind(value, axis, steps):
    count = lax.axis_size(axis)
    initial, last = (max(0, -steps), min(count, count - steps))
    return lax.ppermute(value, axis, [(source, source + steps) for source in range(initial, last)])


def shifted_2(value, axis, by):
    devices = lax.axis_size(axis)
    return lax.ppermute(value, axis, [(i, (i + by) % devices) for i in range(devices)])


def stencil_weights(diffuse, flow_x, flow_y):
    return [
        diffuse + 0.5 * flow_x,
        diffuse - 0.5 * flow_x,
        diffuse + 0.5 * flow_y,
        diffuse - 0.5 * flow_y,
        0.25 * diffuse,
        0.25 * diffuse,
        0.25 * diffuse,
        0.25 * diffuse,
    ]


def eliminate(right_side, coupling_up, coupling_down, initial):

    def advance(state, inputs):
        factor, partial_value = state
        source, upper_term, lower_term = inputs
        divisor = 1.0 + upper_term + lower_term + upper_term * factor
        factor_new = -lower_term / divisor
        partial_new = (source + upper_term * partial_value) / divisor
        return ((factor_new, partial_new), (factor_new, partial_new))

    final_state, outputs = lax.scan(advance, initial, (right_side, coupling_up, coupling_down))
    return outputs


def substitute(factors, partials, below_field):

    def backward(state, inputs):
        factor, partial_value = inputs
        column_value = partial_value - factor * state
        return (column_value, column_value)

    final_state, fields = lax.scan(backward, below_field, (factors, partials), reverse=True)
    return fields


def placing_table():
    cells = []
    for border in range(4):
        for position in range(EDGE):
            cells.append(
                [position, (EDGE - 1) * EDGE + position, position * EDGE, position * EDGE + EDGE - 1][border]
            )
    cells += [0, EDGE - 1, (EDGE - 1) * EDGE, EDGE * EDGE - 1]
    placing = np.zeros((len(cells), EDGE * EDGE), np.float32)
    placing[np.arange(len(cells)), np.array(cells)] = 1.0
    return placing


def embed(field):
    leading = field.shape[:-1]
    square = field.reshape(leading + (EDGE, EDGE))
    padded = jnp.pad(square, [(0, 0)] * len(leading) + [(1, 1), (1, 1)])
    return padded.reshape(leading + ((EDGE + 2) * (EDGE + 2),))


def shards(
    cotangent,
    courant_x,
    courant_y,
    diffusivity,
    vert_diff,
    level_count,
    edge_tile,
    edge_code,
    corner_tile,
    corner_code,
):
    levels_here = cotangent.shape[0]
    tracers = cotangent.shape[1]
    tiles_here = cotangent.shape[2]
    cells = cotangent.shape[3]
    padded_edge = EDGE + 2
    cycle_size = 4 * EDGE + 4
    lev_count = lax.axis_size("lev")
    depth_index = (
        lax.axis_index("lev") * levels_here
        + jnp.arange(levels_here, dtype=jnp.int32)[:, None, None]
    )
    wet_mask = (depth_index < level_count[None]).astype(jnp.float32)
    coupling = jnp.where(depth_index == 0, jnp.float32(0.0), vert_diff * wet_mask)
    deeper = from_behind(coupling[0], "lev", -1)
    coupling_down = jnp.concatenate([coupling[1:], deeper[None]], axis=0)[:, None]
    coupling_up = coupling[:, None]
    initial = (
        jnp.zeros((1, tiles_here, cells), jnp.float32),
        jnp.zeros((tracers, tiles_here, cells), jnp.float32),
    )
    for sweep_index in range(lev_count - 1):
        factors, partials = eliminate(cotangent, coupling_up, coupling_down, initial)
        initial = from_behind((factors[-1], partials[-1]), "lev", 1)
    factors, partials = eliminate(cotangent, coupling_up, coupling_down, initial)
    below_field = jnp.zeros((tracers, tiles_here, cells), jnp.float32)
    for sweep_index in range(lev_count - 1):
        fields = substitute(factors, partials, below_field)
        below_field = from_behind(fields[0], "lev", -1)
    solved = substitute(factors, partials, below_field)
    weighted = solved * wet_mask[:, None]
    weighted_ext = embed(weighted)
    diffuse_ext = embed(diffusivity)[None, None]
    flow_x_ext = embed(courant_x)[:, None]
    flow_y_ext = embed(courant_y)[:, None]
    weights = stencil_weights(diffuse_ext, flow_x_ext, flow_y_ext)
    leading = weighted_ext.shape[:-1]
    spread = jnp.zeros_like(weighted_ext)
    for (shift_row, shift_col), weight in zip(stencil_offsets, weights):
        contribution = weight * weighted_ext
        offset = shift_row * padded_edge + shift_col
        if offset > 0:
            shifted = jnp.concatenate(
                [jnp.zeros(leading + (offset,), jnp.float32), contribution[..., :-offset]], axis=-1
            )
        else:
            shifted = jnp.concatenate(
                [contribution[..., -offset:], jnp.zeros(leading + (-offset,), jnp.float32)], axis=-1
            )
        spread = spread + shifted
    placing = placing_table()
    framed = spread.reshape(leading + (padded_edge, padded_edge))
    outgoing = jnp.concatenate(
        [
            framed[..., 0, 1:-1],
            framed[..., -1, 1:-1],
            framed[..., 1:-1, 0],
            framed[..., 1:-1, -1],
            framed[..., 0, :1],
            framed[..., 0, -1:],
            framed[..., -1, :1],
            framed[..., -1, -1:],
        ],
        axis=-1,
    )
    interior = spread.reshape(leading + (padded_edge, padded_edge))[..., 1:-1, 1:-1].reshape(
        solved.shape
    )
    partners = jnp.concatenate([edge_tile, corner_tile], axis=1)

    def collect(gathered_sum, portion, first_tile):
        tile_span = portion.shape[2]
        onehot = (
            partners[:, :, None]
            == first_tile + jnp.arange(tile_span, dtype=jnp.int32)[None, None, :]
        ).astype(jnp.float32)
        return gathered_sum + jnp.einsum(
            "tkw,dnwr->dntkr", onehot, portion, precision=lax.Precision.HIGHEST
        )

    tile_count = lax.axis_size("tile")
    own_index = lax.axis_index("tile")
    reach = (2 * BAND + tiles_here - 1) // tiles_here
    fetched = collect(
        jnp.zeros((levels_here, tracers, tiles_here, 8, cycle_size), jnp.float32),
        outgoing,
        own_index * tiles_here,
    )
    for distance in range(-reach, reach + 1):
        if distance != 0:
            portion = shifted_2(outgoing, "tile", distance)
            source = (own_index - distance) % tile_count
            fetched = collect(fetched, portion, source * tiles_here)
    side_values = fetched[:, :, :, :4, : 4 * EDGE].reshape(
        levels_here, tracers, tiles_here, 4, 4, EDGE
    )
    side_choice = (
        (edge_code % 4)[:, :, None] == jnp.arange(4, dtype=jnp.int32)[None, None, :]
    ).astype(jnp.float32)
    strips = jnp.sum(side_values * side_choice[None, None, :, :, :, None], axis=4)
    strips = jnp.where((edge_code >= 4)[None, None, :, :, None], strips[..., ::-1], strips)
    corner_values = fetched[:, :, :, 4:, 4 * EDGE :]
    corner_choice = (
        corner_code[:, :, None] == jnp.arange(4, dtype=jnp.int32)[None, None, :]
    ).astype(jnp.float32)
    corner_picked = jnp.sum(corner_values * corner_choice[None, None], axis=4)
    arriving = jnp.concatenate(
        [strips.reshape(levels_here, tracers, tiles_here, 4 * EDGE), corner_picked], axis=3
    )
    returned = jnp.einsum(
        "dntr,rc->dntc", arriving, jnp.asarray(placing), precision=lax.Precision.HIGHEST
    )
    diffuse_here = diffusivity[None, None]
    return wet_mask[:, None] * ((1.0 - 5.0 * diffuse_here) * weighted + interior + returned)


PADDED = 1024
LANES = 128
GROUP = 32
PLANE = 8
MESH = pl.DeviceIdType.MESH
PICK_SEMS = {1: 4, 3: 5, 2: 5, 5: 5, 4: 5, 7: 6, 6: 6}
PICK_GROUPS = [(0, 1), (3, 2, 5, 4), (7, 6)]


def cell_of(lane):
    group, spot = lane // GROUP, lane & (GROUP - 1)
    along = jnp.where(spot < EDGE, spot, 0)
    cell = jnp.where(group == 0, along, (EDGE - 1) * EDGE + along)
    cell = jnp.where(group == 2, EDGE * along, cell)
    cell = jnp.where(group == 3, EDGE * along + EDGE - 1, cell)
    corner = jnp.where(group >= 2, (EDGE - 1) * EDGE, 0) + jnp.where((group & 1) == 1, EDGE - 1, 0)
    return jnp.where(spot < EDGE, cell, jnp.where(spot == EDGE, corner, -1))


def halves(value):
    high = value.astype(jnp.bfloat16)
    return high, (value - high.astype(jnp.float32)).astype(jnp.bfloat16)


def widen(rows):
    return jnp.concatenate(
        [rows, jnp.zeros((rows.shape[0], PADDED - rows.shape[1]), rows.dtype)], axis=1
    )


def exchange_kernel(
    count,
    cot_hbm, cx_hbm, cy_hbm, dif_hbm, vd_hbm, lc_hbm, et_hbm, ec_hbm, ct_hbm, cc_hbm,
    out_ref,
    cot_ref, vdc_ref, cxc_ref, cyc_ref, dif_ref, lc_ref, vd_ref, cx_ref, cy_ref,
    lists_ref, code_ref, pla_ref,
    bcot_ref, bvd_ref, bflow_ref, strips_ref, factor_ref, partial_ref, base_ref,
    tables_ref, table_smem, near_ref, picked_ref, arriving_ref,
    in_sem, send_sem, recv_sem,
):
    levels = cot_ref.shape[0]
    quad = levels // 4
    chunk = levels // PLANE
    cells = cot_ref.shape[2]
    planes = count // PLANE
    slots = 3 * PLANE + 1
    me = lax.axis_index("tile")
    plane = me // PLANE
    here = lax.rem(me, PLANE)

    def start_of(step):
        return PLANE * lax.rem(plane + step + planes, planes)

    mates = [here ^ turn for turn in range(PLANE)]
    own_start = PLANE * plane

    low_end = (planes - plane) // planes
    second_plane = (planes + 1 - plane) // planes * (1 - low_end)
    leap = 1 - 2 * second_plane
    leap_start, other_start = start_of(leap), start_of(-leap)
    turns = [6, 7, 4, 5, 2, 3, 1, 0]

    used = []

    def fetch(pairs, whole):
        sem = in_sem.at[len(used)]
        used.append(whole)
        for source, target in pairs:
            pltpu.make_async_copy(source, target, sem).start()
        return pltpu.make_async_copy(whole, whole, sem)

    def fetch_quads(source, target):
        return fetch(
            [
                (source.at[quad * j : quad * j + quad], target.at[:, 2 * j : 2 * j + 2])
                for j in range(4)
            ],
            target,
        )

    def fetch_flat(source, target):
        return fetch([(source, target.at[2 * n : 2 * n + 2]) for n in range(4)], target)

    def fetch_wide(source, target):
        return fetch([(source, target.at[:, 2 * n : 2 * n + 2]) for n in range(4)], target)

    first = [fetch_quads(vd_hbm, vdc_ref), fetch_flat(lc_hbm, lc_ref)]
    first += [fetch_quads(cx_hbm, cxc_ref), fetch_quads(cy_hbm, cyc_ref), fetch_flat(dif_hbm, dif_ref)]
    half = levels // 2
    second = [
        fetch(
            [
                (cot_hbm.at[half * h : half * h + half, n], cot_ref.at[half * h : half * h + half, 2 * n : 2 * n + 2])
                for n in range(4)
            ],
            cot_ref.at[half * h : half * h + half],
        )
        for h in range(2)
    ]
    first += [fetch([(ec_hbm, code_ref)], code_ref)]
    lists = fetch(
        [(source, lists_ref.at[i]) for i, source in enumerate([et_hbm, ec_hbm, ct_hbm, cc_hbm])],
        lists_ref,
    )
    barrier = pltpu.get_barrier_semaphore()
    peers = [own_start + mates[turn] for turn in turns if turn]
    peers += [start + mates[turn] for start in (leap_start, other_start) for turn in turns]
    for peer in peers:
        pl.semaphore_signal(barrier, inc=1, device_id={"tile": peer}, device_id_type=MESH)

    lane = lax.broadcasted_iota(jnp.int32, (8, LANES), 1)
    row = lax.broadcasted_iota(jnp.int32, (8, LANES), 0)
    parity = row & 1
    group = lane // GROUP
    spot = lane & (GROUP - 1)
    on_side = spot < EDGE

    cells_at = cell_of(lane)
    block_of, lane_of = jnp.where(cells_at < 0, -1, cells_at // LANES), cells_at & (LANES - 1)

    def gather(rows):
        groups = []
        for g in range(rows.shape[0] // 8):
            some = widen(rows[8 * g : 8 * g + 8])
            total = jnp.zeros((8, LANES), rows.dtype)
            for b in range(PADDED // LANES):
                block = jnp.take_along_axis(some[:, LANES * b : LANES * b + LANES], lane_of, axis=1)
                total = jnp.where(block_of == b, block, total)
            groups.append(total)
        return jnp.concatenate(groups, axis=0)

    def spread_rows(values, j):
        return jnp.take_along_axis(values, 2 * j + parity, axis=0)

    for copy in first:
        copy.wait()
    bdepth = gather(lc_ref[...])
    bvd_ref[...] = gather(vdc_ref[...].reshape(8 * quad, cells)).reshape(quad, 8, LANES)

    def bcoupling(k):
        if k == 0 or k == levels:
            return jnp.zeros((8, LANES), jnp.float32)
        return jnp.where(k < bdepth, spread_rows(bvd_ref[k % quad], k // quad), 0.0)

    bdif = gather(dif_ref[...])
    along = gather(cxc_ref[...].reshape(8 * quad, cells)).reshape(quad, 8, LANES)
    across = gather(cyc_ref[...].reshape(8 * quad, cells)).reshape(quad, 8, LANES)
    quarter = 0.25 * bdif
    weight = jnp.where(on_side, bdif, quarter)
    for g in range(quad):
        flow = 0.5 * jnp.where(group < 2, across[g], along[g])
        flow = jnp.where(on_side, jnp.where((group & 1) == 0, flow, -flow), 0.0)
        for j in range(4):
            bflow_ref[quad * j + g] = weight + spread_rows(flow, j)
    code = jnp.zeros((8, LANES), jnp.int32)
    for i in range(2):
        for side in range(4):
            code = jnp.where((parity == i) & (group == side), code_ref[i, side], code)
    turned = jnp.where((code >= 4) & on_side, GROUP * group + (EDGE - 1) - spot, lane)

    middle = levels // 2
    zero = jnp.zeros((8, LANES), jnp.float32)
    coupled = [bcoupling(k) for k in range(levels + 1)]
    inverse, link = [None] * levels, [None] * levels
    excess, low_excess = zero + 1.0, zero + 1.0
    for k in range(middle):
        m = levels - 1 - k
        total, low_total = coupled[k + 1] + excess, coupled[m] + low_excess
        if k < middle - 1:
            inverse[k], inverse[m] = 1.0 / total, 1.0 / low_total
            link[k], link[m] = coupled[k + 1] * inverse[k], coupled[m] * inverse[m]
            excess, low_excess = 1.0 + link[k] * excess, 1.0 + link[m] * low_excess
    joint = coupled[middle]
    meeting = 1.0 / (joint * (excess + low_excess) + excess * low_excess)

    for h in range(2):
        second[h].wait()
        rows = cot_ref[half * h : half * h + half].reshape(8 * half, cells)
        bcot_ref[half * h : half * h + half] = gather(rows).reshape(half, 8, LANES)
    fourth = [fetch_wide(vd_hbm, vd_ref)]
    fifth = [fetch_wide(cx_hbm, cx_ref), fetch_wide(cy_hbm, cy_ref)]
    value = [None] * levels
    part, low_part = zero, zero
    for k in range(middle):
        m = levels - 1 - k
        source = bcot_ref[k] + coupled[k] * part
        low_source = bcot_ref[m] + coupled[m + 1] * low_part
        if k < middle - 1:
            part, low_part = source * inverse[k], low_source * inverse[m]
            value[k], value[m] = part, low_part
    value[middle] = (low_source * total + joint * source) * meeting
    value[middle - 1] = (source * low_total + joint * low_source) * meeting
    for k in range(middle - 2, -1, -1):
        m = levels - 1 - k
        value[k] = value[k] + link[k] * value[k + 1]
        value[m] = value[m] + link[m] * value[m - 1]
    for k in range(levels):
        u = jnp.where(k < bdepth, value[k], 0.0)
        diagonal = jnp.where(on_side, quarter * u, 0.0)
        beside = pltpu.roll(diagonal, 1, 1) + pltpu.roll(diagonal, LANES - 1, 1)
        halo = bflow_ref[k] * u + jnp.where(on_side, beside, 0.0)
        strips_ref[k] = jnp.take_along_axis(halo, turned, axis=1)

    lists.wait()
    tile_index = lax.broadcasted_iota(jnp.int32, (2, 4), 0)
    side_index = lax.broadcasted_iota(jnp.int32, (2, 4), 1)
    tables_ref[here] = jnp.zeros((8, LANES), jnp.int32)
    for part_index in range(2):
        tile, kind = lists_ref[2 * part_index], lists_ref[2 * part_index + 1]
        device = tile >> 1
        step = device // PLANE - plane + 1
        step = jnp.where(step < 0, step + planes, step)
        step = jnp.where(step >= planes, step - planes, step)
        slot = PLANE * step + (device & (PLANE - 1))
        slot = jnp.where((tile < 0) | (step > 2), 3 * PLANE, slot)
        swapped = (tile & 1) ^ tile_index
        shift = GROUP * ((side_index - (kind & 3)) & 3)
        tables_ref[here, 2 * part_index : 2 * part_index + 2, 0:4] = slots * swapped + slot
        tables_ref[here, 2 * part_index + 4 : 2 * part_index + 6, 0:4] = shift

    pl.semaphore_wait(barrier, len(peers))

    def send(step, start, some):
        mark = PLANE * (1 - step) + here
        for turn in some:
            pltpu.make_async_remote_copy(
                src_ref=strips_ref.at[pl.ds(chunk * mates[turn], chunk)],
                dst_ref=near_ref.at[mark],
                send_sem=send_sem.at[0],
                recv_sem=recv_sem.at[1 - step],
                device_id={"tile": start + mates[turn]},
                device_id_type=MESH,
            ).start()

    def whole(source, target, mark):
        return pltpu.make_async_remote_copy(
            src_ref=source,
            dst_ref=target,
            send_sem=send_sem.at[mark],
            recv_sem=recv_sem.at[mark],
            device_id={"tile": own_start + mates[1]},
            device_id_type=MESH,
        )

    @pl.when(low_end == 1)
    def _():
        send(0, own_start, turns[:-1])
        send(leap, leap_start, turns)
        send(-leap, other_start, turns)

    @pl.when(low_end == 0)
    def _():
        send(leap, leap_start, turns)
        send(0, own_start, turns[:-1])
        send(-leap, other_start, turns)

    for turn in turns[:-1]:
        pltpu.make_async_remote_copy(
            src_ref=tables_ref.at[here],
            dst_ref=tables_ref.at[here],
            send_sem=send_sem.at[3],
            recv_sem=recv_sem.at[3],
            device_id={"tile": own_start + mates[turn]},
            device_id_type=MESH,
        ).start()
    near_ref[PLANE + here] = strips_ref[pl.ds(chunk * here, chunk)]
    for slot in (slots - 1, 2 * slots - 1):
        near_ref[slot] = jnp.zeros((chunk, 8, LANES), jnp.float32)

    spots = lax.broadcasted_iota(jnp.int32, (LANES, PADDED), 1)
    cells_at = cell_of(lax.broadcasted_iota(jnp.int32, (LANES, 1), 0))
    placer = jnp.where(spots == cells_at, 1.0, 0.0).astype(jnp.bfloat16)
    pla_ref[0:LANES] = placer
    pla_ref[LANES:] = placer
    for copy in fourth:
        copy.wait()
    depth = lc_ref[...]

    def advance(k, state):
        up, excess, part = state
        later = jnp.minimum(k + 1, levels - 1)
        down = jnp.where(k + 1 < depth, vd_ref[later], 0.0)
        down = jnp.where(k + 1 < levels, down, 0.0)
        inverse = 1.0 / (down + excess)
        factor = down * inverse
        part = (cot_ref[k] + up * part) * inverse
        factor_ref[k] = factor
        partial_ref[k] = part
        return down, 1.0 + factor * excess, part

    blank = jnp.zeros((8, cells), jnp.float32)
    lax.fori_loop(0, levels, advance, (blank, blank + 1.0, blank), unroll=2)

    for copy in fifth:
        copy.wait()
    wide_lane = lax.broadcasted_iota(jnp.int32, (8, PADDED), 1)
    wraps = PADDED - EDGE
    column = lax.rem(jnp.where(wide_lane >= wraps, wide_lane - wraps, wide_lane), EDGE)
    not_first = column != 0
    not_last = column != EDGE - 1
    diffuse = widen(dif_ref[...])
    quarter_wide = 0.25 * diffuse
    centre = 1.0 - 5.0 * diffuse
    wide_depth = widen(depth)

    def substitute_back(step, solved):
        k = levels - 1 - step
        solved = partial_ref[k] + factor_ref[k] * solved
        u = widen(jnp.where(k < depth, solved, 0.0))
        half_x = 0.5 * widen(cx_ref[k])
        half_y = 0.5 * widen(cy_ref[k])
        diagonal = quarter_wide * u
        both = pltpu.roll(diagonal, EDGE, 1) + pltpu.roll(diagonal, PADDED - EDGE, 1)
        west = both + (diffuse + half_x) * u
        east = both + (diffuse - half_x) * u
        total = pltpu.roll((diffuse + half_y) * u, PADDED - EDGE, 1)
        total = total + pltpu.roll((diffuse - half_y) * u, EDGE, 1)
        total = total + pltpu.roll(jnp.where(not_first, west, 0.0), PADDED - 1, 1)
        total = total + pltpu.roll(jnp.where(not_last, east, 0.0), 1, 1)
        base_ref[k] = jnp.where(k < wide_depth, centre * u + total, 0.0)
        return solved

    lax.fori_loop(0, levels, substitute_back, blank, unroll=2)

    others = pl.ds(0, PLANE - 1)
    told = whole(tables_ref.at[others], tables_ref.at[others], 3)
    told.wait_recv()
    to_smem = pltpu.make_async_copy(tables_ref, table_smem, in_sem.at[len(used)])
    to_smem.start()

    for below in (1, 2, 0):
        group_slots = PLANE - 1 if below == 1 else PLANE
        some = near_ref.at[pl.ds(PLANE * below, group_slots)]
        whole(some, some, below).wait_recv()
        for slot in range(PLANE * below, PLANE * below + PLANE):
            for t in range(chunk):
                near_ref[slots + slot, t] = jnp.take_along_axis(near_ref[slot, t], row ^ 1, axis=0)
    to_smem.wait()

    chosen = [[(wanted & (group == side))[None] for side in range(4)] for wanted in (on_side, spot == EDGE)]
    for turn in turns:
        pair = []
        for i in range(2):
            total = jnp.zeros((chunk, 8, LANES), jnp.float32)
            for kind in range(2):
                for side in range(4):
                    values = near_ref[table_smem[mates[turn], 2 * kind + i, side]]
                    values = pltpu.roll(values, table_smem[mates[turn], 2 * kind + i + 4, side], 2)
                    total = jnp.where(chosen[kind][side], values, total)
            pair.append(total)
        total = jnp.where((parity == 0)[None], pair[0], pair[1])
        if turn == 0:
            arriving_ref[pl.ds(chunk * here, chunk)] = total
            continue
        picked_ref[turn - 1] = total
        pltpu.make_async_remote_copy(
            src_ref=picked_ref.at[turn - 1],
            dst_ref=arriving_ref.at[pl.ds(chunk * here, chunk)],
            send_sem=send_sem.at[4],
            recv_sem=recv_sem.at[PICK_SEMS[turn]],
            device_id={"tile": own_start + mates[turn]},
            device_id_type=MESH,
        ).start()

    for members in PICK_GROUPS:
        some = arriving_ref.at[pl.ds(0, chunk * len([turn for turn in members if turn]))]
        whole(some, some, PICK_SEMS[members[-1]]).wait_recv()
        places = [chunk * mates[turn] + t for turn in members for t in range(chunk)]
        rows = [jnp.where(k < bdepth, arriving_ref[k], 0.0) for k in places]
        high, low = halves(jnp.concatenate(rows, axis=0))
        returned = jnp.dot(
            jnp.concatenate([high, low], axis=1), pla_ref[...], preferred_element_type=jnp.float32
        )
        for n, k in enumerate(places):
            result = base_ref[k] + returned[8 * n : 8 * n + 8]
            out_ref[k] = result[:, :cells]
    every = near_ref.at[pl.ds(0, 3 * PLANE - 1)]
    whole(every, every, 0).wait_send()
    told.wait_send()
    whole(picked_ref, picked_ref, 4).wait_send()


def store_kernel(held_ref, out_hbm, sem):
    for n in range(4):
        pltpu.make_async_copy(held_ref.at[:, 2 * n : 2 * n + 2], out_hbm.at[:, n], sem).start()
    pltpu.make_async_copy(out_hbm, out_hbm, sem).wait()


def shards_fast(
    cotangent,
    courant_x,
    courant_y,
    diffusivity,
    vert_diff,
    level_count,
    edge_tile,
    edge_code,
    corner_tile,
    corner_code,
):
    levels, tracers, tiles_here, cells = cotangent.shape
    count = lax.axis_size("tile")
    vmem = pl.BlockSpec(memory_space=pltpu.VMEM)
    hbm = pl.BlockSpec(memory_space=pltpu.HBM)
    chunk = levels // PLANE
    f32 = jnp.float32
    held = pl.pallas_call(
        functools.partial(exchange_kernel, count),
        name="exchange",
        out_shape=pltpu.VMEM((levels, 8, cells), f32),
        in_specs=[hbm] * 10,
        out_specs=vmem,
        scratch_shapes=[
            pltpu.VMEM((levels, 8, cells), f32),
            pltpu.VMEM((levels // 4, 8, cells), f32),
            pltpu.VMEM((levels // 4, 8, cells), f32),
            pltpu.VMEM((levels // 4, 8, cells), f32),
            pltpu.VMEM((8, cells), f32),
            pltpu.VMEM((8, cells), jnp.int32),
            pltpu.VMEM((levels, 8, cells), f32),
            pltpu.VMEM((levels, 8, cells), f32),
            pltpu.VMEM((levels, 8, cells), f32),
            pltpu.VMEM((4, 2, 4), jnp.int32),
            pltpu.SMEM((2, 4), jnp.int32),
            pltpu.VMEM((2 * LANES, PADDED), jnp.bfloat16),
            pltpu.VMEM((levels, 8, LANES), f32),
            pltpu.VMEM((levels // 4, 8, LANES), f32),
            pltpu.VMEM((levels, 8, LANES), f32),
            pltpu.VMEM((levels, 8, LANES), f32),
            pltpu.VMEM((levels, 8, cells), f32),
            pltpu.VMEM((levels, 8, cells), f32),
            pltpu.VMEM((levels, 8, PADDED), f32),
            pltpu.VMEM((PLANE, 8, LANES), jnp.int32),
            pltpu.SMEM((PLANE, 8, LANES), jnp.int32),
            pltpu.VMEM((2 * (3 * PLANE + 1), chunk, 8, LANES), f32),
            pltpu.VMEM((PLANE - 1, chunk, 8, LANES), f32),
            pltpu.VMEM((levels, 8, LANES), f32),
            pltpu.SemaphoreType.DMA((13,)),
            pltpu.SemaphoreType.DMA((7,)),
            pltpu.SemaphoreType.DMA((7,)),
        ],
        compiler_params=pltpu.CompilerParams(
            collective_id=0, has_side_effects=True, vmem_limit_bytes=62 << 20
        ),
    )(
        cotangent, courant_x, courant_y, diffusivity, vert_diff, level_count,
        edge_tile, edge_code, corner_tile, corner_code,
    )
    return pl.pallas_call(
        store_kernel,
        name="store",
        out_shape=jax.ShapeDtypeStruct(cotangent.shape, f32),
        in_specs=[vmem],
        out_specs=hbm,
        scratch_shapes=[pltpu.SemaphoreType.DMA],
        compiler_params=pltpu.CompilerParams(vmem_limit_bytes=8 << 20),
    )(held)


def solution(mesh):
    placed = (
        P("lev", None, "tile", None),
        P("lev", "tile", None),
        P("lev", "tile", None),
        P("tile", None),
        P("lev", "tile", None),
        P("tile", None),
        P("tile", None),
        P("tile", None),
        P("tile", None),
        P("tile", None),
    )
    fast = mesh.shape["lev"] == 1 and mesh.shape["tile"] % PLANE == 0 and mesh.shape["tile"] > 2 * BAND
    return jax.shard_map(
        shards_fast if fast else shards, mesh=mesh, in_specs=placed, out_specs=P("lev", None, "tile", None), check_vma=False
    )
```

```python
import functools

import jax
import jax.numpy as jnp
import numpy as np
from jax import lax
from jax.experimental import pallas as pl
from jax.experimental.pallas import tpu as pltpu
from jax.sharding import PartitionSpec as P

EDGE = 30
BAND = 8


stencil_offsets = [(0, -1), (0, 1), (-1, 0), (1, 0), (-1, -1), (-1, 1), (1, -1), (1, 1)]


def from_behind(value, axis, steps):
    count = lax.axis_size(axis)
    initial, last = (max(0, -steps), min(count, count - steps))
    return lax.ppermute(value, axis, [(source, source + steps) for source in range(initial, last)])


def shifted_2(value, axis, by):
    devices = lax.axis_size(axis)
    return lax.ppermute(value, axis, [(i, (i + by) % devices) for i in range(devices)])


def stencil_weights(diffuse, flow_x, flow_y):
    return [
        diffuse + 0.5 * flow_x,
        diffuse - 0.5 * flow_x,
        diffuse + 0.5 * flow_y,
        diffuse - 0.5 * flow_y,
        0.25 * diffuse,
        0.25 * diffuse,
        0.25 * diffuse,
        0.25 * diffuse,
    ]


def eliminate(right_side, coupling_up, coupling_down, initial):

    def advance(state, inputs):
        factor, partial_value = state
        source, upper_term, lower_term = inputs
        divisor = 1.0 + upper_term + lower_term + upper_term * factor
        factor_new = -lower_term / divisor
        partial_new = (source + upper_term * partial_value) / divisor
        return ((factor_new, partial_new), (factor_new, partial_new))

    final_state, outputs = lax.scan(advance, initial, (right_side, coupling_up, coupling_down))
    return outputs


def substitute(factors, partials, below_field):

    def backward(state, inputs):
        factor, partial_value = inputs
        column_value = partial_value - factor * state
        return (column_value, column_value)

    final_state, fields = lax.scan(backward, below_field, (factors, partials), reverse=True)
    return fields


def placing_table():
    cells = []
    for border in range(4):
        for position in range(EDGE):
            cells.append(
                [position, (EDGE - 1) * EDGE + position, position * EDGE, position * EDGE + EDGE - 1][border]
            )
    cells += [0, EDGE - 1, (EDGE - 1) * EDGE, EDGE * EDGE - 1]
    placing = np.zeros((len(cells), EDGE * EDGE), np.float32)
    placing[np.arange(len(cells)), np.array(cells)] = 1.0
    return placing


def embed(field):
    leading = field.shape[:-1]
    square = field.reshape(leading + (EDGE, EDGE))
    padded = jnp.pad(square, [(0, 0)] * len(leading) + [(1, 1), (1, 1)])
    return padded.reshape(leading + ((EDGE + 2) * (EDGE + 2),))


def shards(
    cotangent,
    courant_x,
    courant_y,
    diffusivity,
    vert_diff,
    level_count,
    edge_tile,
    edge_code,
    corner_tile,
    corner_code,
):
    levels_here = cotangent.shape[0]
    tracers = cotangent.shape[1]
    tiles_here = cotangent.shape[2]
    cells = cotangent.shape[3]
    padded_edge = EDGE + 2
    cycle_size = 4 * EDGE + 4
    lev_count = lax.axis_size("lev")
    depth_index = (
        lax.axis_index("lev") * levels_here
        + jnp.arange(levels_here, dtype=jnp.int32)[:, None, None]
    )
    wet_mask = (depth_index < level_count[None]).astype(jnp.float32)
    coupling = jnp.where(depth_index == 0, jnp.float32(0.0), vert_diff * wet_mask)
    deeper = from_behind(coupling[0], "lev", -1)
    coupling_down = jnp.concatenate([coupling[1:], deeper[None]], axis=0)[:, None]
    coupling_up = coupling[:, None]
    initial = (
        jnp.zeros((1, tiles_here, cells), jnp.float32),
        jnp.zeros((tracers, tiles_here, cells), jnp.float32),
    )
    for sweep_index in range(lev_count - 1):
        factors, partials = eliminate(cotangent, coupling_up, coupling_down, initial)
        initial = from_behind((factors[-1], partials[-1]), "lev", 1)
    factors, partials = eliminate(cotangent, coupling_up, coupling_down, initial)
    below_field = jnp.zeros((tracers, tiles_here, cells), jnp.float32)
    for sweep_index in range(lev_count - 1):
        fields = substitute(factors, partials, below_field)
        below_field = from_behind(fields[0], "lev", -1)
    solved = substitute(factors, partials, below_field)
    weighted = solved * wet_mask[:, None]
    weighted_ext = embed(weighted)
    diffuse_ext = embed(diffusivity)[None, None]
    flow_x_ext = embed(courant_x)[:, None]
    flow_y_ext = embed(courant_y)[:, None]
    weights = stencil_weights(diffuse_ext, flow_x_ext, flow_y_ext)
    leading = weighted_ext.shape[:-1]
    spread = jnp.zeros_like(weighted_ext)
    for (shift_row, shift_col), weight in zip(stencil_offsets, weights):
        contribution = weight * weighted_ext
        offset = shift_row * padded_edge + shift_col
        if offset > 0:
            shifted = jnp.concatenate(
                [jnp.zeros(leading + (offset,), jnp.float32), contribution[..., :-offset]], axis=-1
            )
        else:
            shifted = jnp.concatenate(
                [contribution[..., -offset:], jnp.zeros(leading + (-offset,), jnp.float32)], axis=-1
            )
        spread = spread + shifted
    placing = placing_table()
    framed = spread.reshape(leading + (padded_edge, padded_edge))
    outgoing = jnp.concatenate(
        [
            framed[..., 0, 1:-1],
            framed[..., -1, 1:-1],
            framed[..., 1:-1, 0],
            framed[..., 1:-1, -1],
            framed[..., 0, :1],
            framed[..., 0, -1:],
            framed[..., -1, :1],
            framed[..., -1, -1:],
        ],
        axis=-1,
    )
    interior = spread.reshape(leading + (padded_edge, padded_edge))[..., 1:-1, 1:-1].reshape(
        solved.shape
    )
    partners = jnp.concatenate([edge_tile, corner_tile], axis=1)

    def collect(gathered_sum, portion, first_tile):
        tile_span = portion.shape[2]
        onehot = (
            partners[:, :, None]
            == first_tile + jnp.arange(tile_span, dtype=jnp.int32)[None, None, :]
        ).astype(jnp.float32)
        return gathered_sum + jnp.einsum(
            "tkw,dnwr->dntkr", onehot, portion, precision=lax.Precision.HIGHEST
        )

    tile_count = lax.axis_size("tile")
    own_index = lax.axis_index("tile")
    reach = (2 * BAND + tiles_here - 1) // tiles_here
    fetched = collect(
        jnp.zeros((levels_here, tracers, tiles_here, 8, cycle_size), jnp.float32),
        outgoing,
        own_index * tiles_here,
    )
    for distance in range(-reach, reach + 1):
        if distance != 0:
            portion = shifted_2(outgoing, "tile", distance)
            source = (own_index - distance) % tile_count
            fetched = collect(fetched, portion, source * tiles_here)
    side_values = fetched[:, :, :, :4, : 4 * EDGE].reshape(
        levels_here, tracers, tiles_here, 4, 4, EDGE
    )
    side_choice = (
        (edge_code % 4)[:, :, None] == jnp.arange(4, dtype=jnp.int32)[None, None, :]
    ).astype(jnp.float32)
    strips = jnp.sum(side_values * side_choice[None, None, :, :, :, None], axis=4)
    strips = jnp.where((edge_code >= 4)[None, None, :, :, None], strips[..., ::-1], strips)
    corner_values = fetched[:, :, :, 4:, 4 * EDGE :]
    corner_choice = (
        corner_code[:, :, None] == jnp.arange(4, dtype=jnp.int32)[None, None, :]
    ).astype(jnp.float32)
    corner_picked = jnp.sum(corner_values * corner_choice[None, None], axis=4)
    arriving = jnp.concatenate(
        [strips.reshape(levels_here, tracers, tiles_here, 4 * EDGE), corner_picked], axis=3
    )
    returned = jnp.einsum(
        "dntr,rc->dntc", arriving, jnp.asarray(placing), precision=lax.Precision.HIGHEST
    )
    diffuse_here = diffusivity[None, None]
    return wet_mask[:, None] * ((1.0 - 5.0 * diffuse_here) * weighted + interior + returned)


PADDED = 1024
LANES = 128
GROUP = 32
PLANE = 8
MESH = pl.DeviceIdType.MESH
SEND_SEMS = (0, 0, 0, 1, 2, 2, 2)
PICK_SEMS = {1: 4, 3: 5, 2: 5, 5: 5, 4: 5, 7: 6, 6: 6}
PICK_GROUPS = [(0, 1), (3, 2, 5, 4), (7, 6)]


def cell_of(lane):
    group, spot = lane // GROUP, lane & (GROUP - 1)
    along = jnp.where(spot < EDGE, spot, 0)
    cell = jnp.where(group == 0, along, (EDGE - 1) * EDGE + along)
    cell = jnp.where(group == 2, EDGE * along, cell)
    cell = jnp.where(group == 3, EDGE * along + EDGE - 1, cell)
    corner = jnp.where(group >= 2, (EDGE - 1) * EDGE, 0) + jnp.where((group & 1) == 1, EDGE - 1, 0)
    return jnp.where(spot < EDGE, cell, jnp.where(spot == EDGE, corner, -1))


def halves(value):
    high = value.astype(jnp.bfloat16)
    return high, (value - high.astype(jnp.float32)).astype(jnp.bfloat16)


def widen(rows):
    return jnp.concatenate(
        [rows, jnp.zeros((rows.shape[0], PADDED - rows.shape[1]), rows.dtype)], axis=1
    )


def exchange_kernel(
    count,
    cot_hbm, cx_hbm, cy_hbm, dif_hbm, vd_hbm, lc_hbm, et_hbm, ec_hbm, ct_hbm, cc_hbm,
    out_ref,
    cot_ref, quads_ref, dif_ref, lc_ref, wide_ref,
    lists_ref, code_ref, pla_ref,
    bcot_ref, bvd_ref, bflow_ref, strips_ref, factor_ref, partial_ref, base_ref,
    tables_ref, table_smem, near_ref, picked_ref, arriving_ref,
    in_sem, send_sem, recv_sem,
):
    levels = cot_ref.shape[0]
    quad = levels // 4
    chunk = levels // PLANE
    cells = cot_ref.shape[2]
    planes = count // PLANE
    slots = 3 * PLANE + 1
    me = lax.axis_index("tile")
    plane = me // PLANE
    here = lax.rem(me, PLANE)

    def start_of(step):
        return PLANE * lax.rem(plane + step + planes, planes)

    mates = [here ^ turn for turn in range(PLANE)]
    own_start = PLANE * plane

    low_end = (planes - plane) // planes
    second_plane = (planes + 1 - plane) // planes * (1 - low_end)
    leap = 1 - 2 * second_plane
    leap_start, other_start = start_of(leap), start_of(-leap)
    turns = [6, 7, 4, 5, 2, 3, 1, 0]

    used = []

    def fetch(pairs, whole):
        sem = in_sem.at[len(used)]
        used.append(whole)
        for source, target in pairs:
            pltpu.make_async_copy(source, target, sem).start()
        return pltpu.make_async_copy(whole, whole, sem)

    def fetch_flat(source, target):
        return fetch([(source, target.at[2 * n : 2 * n + 2]) for n in range(4)], target)

    columns = [vd_hbm, cx_hbm, cy_hbm]
    first = [
        fetch(
            [
                (source.at[quad * j : quad * j + quad], quads_ref.at[i, :, 2 * j : 2 * j + 2])
                for i, source in enumerate(columns)
                for j in range(4)
            ],
            quads_ref,
        ),
        fetch_flat(lc_hbm, lc_ref),
    ]
    second = fetch([(cot_hbm.at[:, n], cot_ref.at[:, 2 * n : 2 * n + 2]) for n in range(4)], cot_ref)
    first += [fetch_flat(dif_hbm, dif_ref), fetch([(ec_hbm, code_ref)], code_ref)]
    lists = fetch(
        [(source, lists_ref.at[i]) for i, source in enumerate([et_hbm, ec_hbm, ct_hbm, cc_hbm])],
        lists_ref,
    )
    barrier = pltpu.get_barrier_semaphore()
    peers = [own_start + mates[turn] for turn in turns if turn]
    peers += [start + mates[turn] for start in (leap_start, other_start) for turn in turns]
    for peer in peers:
        pl.semaphore_signal(barrier, inc=1, device_id={"tile": peer}, device_id_type=MESH)

    lane = lax.broadcasted_iota(jnp.int32, (8, LANES), 1)
    row = lax.broadcasted_iota(jnp.int32, (8, LANES), 0)
    parity = row & 1
    group = lane // GROUP
    spot = lane & (GROUP - 1)
    on_side = spot < EDGE

    cells_at = cell_of(lane)
    block_of, lane_of = jnp.where(cells_at < 0, -1, cells_at // LANES), cells_at & (LANES - 1)

    def gather(rows):
        groups = []
        for g in range(rows.shape[0] // 8):
            some = widen(rows[8 * g : 8 * g + 8])
            total = jnp.zeros((8, LANES), rows.dtype)
            for b in range(PADDED // LANES):
                block = jnp.take_along_axis(some[:, LANES * b : LANES * b + LANES], lane_of, axis=1)
                total = jnp.where(block_of == b, block, total)
            groups.append(total)
        return jnp.concatenate(groups, axis=0)

    def spread_rows(values, j):
        return jnp.take_along_axis(values, 2 * j + parity, axis=0)

    for copy in first:
        copy.wait()
    bdepth = gather(lc_ref[...])
    bvd_ref[...] = gather(quads_ref[0].reshape(8 * quad, cells)).reshape(quad, 8, LANES)

    def bcoupling(k):
        if k == 0 or k == levels:
            return jnp.zeros((8, LANES), jnp.float32)
        return jnp.where(k < bdepth, spread_rows(bvd_ref[k % quad], k // quad), 0.0)

    bdif = gather(dif_ref[...])
    along = gather(quads_ref[1].reshape(8 * quad, cells)).reshape(quad, 8, LANES)
    across = gather(quads_ref[2].reshape(8 * quad, cells)).reshape(quad, 8, LANES)
    quarter = 0.25 * bdif
    weight = jnp.where(on_side, bdif, quarter)
    for g in range(quad):
        flow = 0.5 * jnp.where(group < 2, across[g], along[g])
        flow = jnp.where(on_side, jnp.where((group & 1) == 0, flow, -flow), 0.0)
        for j in range(4):
            bflow_ref[quad * j + g] = weight + spread_rows(flow, j)
    code = jnp.zeros((8, LANES), jnp.int32)
    for i in range(2):
        for side in range(4):
            code = jnp.where((parity == i) & (group == side), code_ref[i, side], code)
    turned = jnp.where((code >= 4) & on_side, GROUP * group + (EDGE - 1) - spot, lane)

    middle = levels // 2
    zero = jnp.zeros((8, LANES), jnp.float32)
    coupled = [bcoupling(k) for k in range(levels + 1)]
    inverse, link = [None] * levels, [None] * levels
    excess, low_excess = zero + 1.0, zero + 1.0
    for k in range(middle):
        m = levels - 1 - k
        total, low_total = coupled[k + 1] + excess, coupled[m] + low_excess
        if k < middle - 1:
            inverse[k], inverse[m] = 1.0 / total, 1.0 / low_total
            link[k], link[m] = coupled[k + 1] * inverse[k], coupled[m] * inverse[m]
            excess, low_excess = 1.0 + link[k] * excess, 1.0 + link[m] * low_excess
    joint = coupled[middle]
    meeting = 1.0 / (joint * (excess + low_excess) + excess * low_excess)

    second.wait()
    bcot_ref[...] = gather(cot_ref[...].reshape(8 * levels, cells)).reshape(levels, 8, LANES)
    wide = fetch(
        [
            (source, wide_ref.at[i, :, 2 * n : 2 * n + 2])
            for i, source in enumerate(columns)
            for n in range(4)
        ],
        wide_ref,
    )
    value = [None] * levels
    part, low_part = zero, zero
    for k in range(middle):
        m = levels - 1 - k
        source = bcot_ref[k] + coupled[k] * part
        low_source = bcot_ref[m] + coupled[m + 1] * low_part
        if k < middle - 1:
            part, low_part = source * inverse[k], low_source * inverse[m]
            value[k], value[m] = part, low_part
    value[middle] = (low_source * total + joint * source) * meeting
    value[middle - 1] = (source * low_total + joint * low_source) * meeting
    for k in range(middle - 2, -1, -1):
        m = levels - 1 - k
        value[k] = value[k] + link[k] * value[k + 1]
        value[m] = value[m] + link[m] * value[m - 1]
    for k in range(levels):
        u = jnp.where(k < bdepth, value[k], 0.0)
        diagonal = jnp.where(on_side, quarter * u, 0.0)
        beside = pltpu.roll(diagonal, 1, 1) + pltpu.roll(diagonal, LANES - 1, 1)
        halo = bflow_ref[k] * u + jnp.where(on_side, beside, 0.0)
        strips_ref[k] = jnp.take_along_axis(halo, turned, axis=1)

    lists.wait()
    tile_index = lax.broadcasted_iota(jnp.int32, (2, 4), 0)
    side_index = lax.broadcasted_iota(jnp.int32, (2, 4), 1)
    tables_ref[here] = jnp.zeros((8, LANES), jnp.int32)
    for part_index in range(2):
        tile, kind = lists_ref[2 * part_index], lists_ref[2 * part_index + 1]
        device = tile >> 1
        step = device // PLANE - plane + 1
        step = jnp.where(step < 0, step + planes, step)
        step = jnp.where(step >= planes, step - planes, step)
        slot = PLANE * step + (device & (PLANE - 1))
        slot = jnp.where((tile < 0) | (step > 2), 3 * PLANE, slot)
        swapped = (tile & 1) ^ tile_index
        shift = GROUP * ((side_index - (kind & 3)) & 3)
        tables_ref[here, 2 * part_index : 2 * part_index + 2, 0:4] = slots * swapped + slot
        tables_ref[here, 2 * part_index + 4 : 2 * part_index + 6, 0:4] = shift

    pl.semaphore_wait(barrier, len(peers))

    def send(step, start, some):
        mark = PLANE * (1 - step) + here
        for turn in some:
            pltpu.make_async_remote_copy(
                src_ref=strips_ref.at[pl.ds(chunk * mates[turn], chunk)],
                dst_ref=near_ref.at[mark],
                send_sem=send_sem.at[0],
                recv_sem=recv_sem.at[1 - step],
                device_id={"tile": start + mates[turn]},
                device_id_type=MESH,
            ).start()

    def whole(source, target, mark):
        return pltpu.make_async_remote_copy(
            src_ref=source,
            dst_ref=target,
            send_sem=send_sem.at[SEND_SEMS[mark]],
            recv_sem=recv_sem.at[mark],
            device_id={"tile": own_start + mates[1]},
            device_id_type=MESH,
        )

    @pl.when(low_end == 1)
    def _():
        send(0, own_start, turns[:-1])
        send(leap, leap_start, turns)
        send(-leap, other_start, turns)

    @pl.when(low_end == 0)
    def _():
        send(leap, leap_start, turns)
        send(0, own_start, turns[:-1])
        send(-leap, other_start, turns)

    for turn in turns[:-1]:
        pltpu.make_async_remote_copy(
            src_ref=tables_ref.at[here],
            dst_ref=tables_ref.at[here],
            send_sem=send_sem.at[1],
            recv_sem=recv_sem.at[3],
            device_id={"tile": own_start + mates[turn]},
            device_id_type=MESH,
        ).start()
    near_ref[PLANE + here] = strips_ref[pl.ds(chunk * here, chunk)]
    for slot in (slots - 1, 2 * slots - 1):
        near_ref[slot] = jnp.zeros((chunk, 8, LANES), jnp.float32)

    spots = lax.broadcasted_iota(jnp.int32, (LANES, PADDED), 1)
    cells_at = cell_of(lax.broadcasted_iota(jnp.int32, (LANES, 1), 0))
    placer = jnp.where(spots == cells_at, 1.0, 0.0).astype(jnp.bfloat16)
    pla_ref[0:LANES] = placer
    pla_ref[LANES:] = placer
    wide.wait()
    depth = lc_ref[...]

    def advance(k, state):
        up, excess, part = state
        later = jnp.minimum(k + 1, levels - 1)
        down = jnp.where(k + 1 < depth, wide_ref[0, later], 0.0)
        down = jnp.where(k + 1 < levels, down, 0.0)
        inverse = 1.0 / (down + excess)
        factor = down * inverse
        part = (cot_ref[k] + up * part) * inverse
        factor_ref[k] = factor
        partial_ref[k] = part
        return down, 1.0 + factor * excess, part

    blank = jnp.zeros((8, cells), jnp.float32)
    lax.fori_loop(0, levels, advance, (blank, blank + 1.0, blank), unroll=2)

    wide_lane = lax.broadcasted_iota(jnp.int32, (8, PADDED), 1)
    wraps = PADDED - EDGE
    column = lax.rem(jnp.where(wide_lane >= wraps, wide_lane - wraps, wide_lane), EDGE)
    not_first = column != 0
    not_last = column != EDGE - 1
    diffuse = widen(dif_ref[...])
    quarter_wide = 0.25 * diffuse
    centre = 1.0 - 5.0 * diffuse
    wide_depth = widen(depth)

    def substitute_back(step, solved):
        k = levels - 1 - step
        solved = partial_ref[k] + factor_ref[k] * solved
        u = widen(jnp.where(k < depth, solved, 0.0))
        half_x = 0.5 * widen(wide_ref[1, k])
        half_y = 0.5 * widen(wide_ref[2, k])
        diagonal = quarter_wide * u
        both = pltpu.roll(diagonal, EDGE, 1) + pltpu.roll(diagonal, PADDED - EDGE, 1)
        west = both + (diffuse + half_x) * u
        east = both + (diffuse - half_x) * u
        total = pltpu.roll((diffuse + half_y) * u, PADDED - EDGE, 1)
        total = total + pltpu.roll((diffuse - half_y) * u, EDGE, 1)
        total = total + pltpu.roll(jnp.where(not_first, west, 0.0), PADDED - 1, 1)
        total = total + pltpu.roll(jnp.where(not_last, east, 0.0), 1, 1)
        base_ref[k] = jnp.where(k < wide_depth, centre * u + total, 0.0)
        return solved

    lax.fori_loop(0, levels, substitute_back, blank, unroll=2)

    others = pl.ds(0, PLANE - 1)
    told = whole(tables_ref.at[others], tables_ref.at[others], 3)
    told.wait_recv()
    to_smem = pltpu.make_async_copy(tables_ref, table_smem, in_sem.at[len(used)])
    to_smem.start()

    for below in (1, 2, 0):
        group_slots = PLANE - 1 if below == 1 else PLANE
        some = near_ref.at[pl.ds(PLANE * below, group_slots)]
        whole(some, some, below).wait_recv()
        for slot in range(PLANE * below, PLANE * below + PLANE):
            for t in range(chunk):
                near_ref[slots + slot, t] = jnp.take_along_axis(near_ref[slot, t], row ^ 1, axis=0)
    to_smem.wait()

    chosen = [[(wanted & (group == side))[None] for side in range(4)] for wanted in (on_side, spot == EDGE)]
    for turn in turns:
        pair = []
        for i in range(2):
            total = jnp.zeros((chunk, 8, LANES), jnp.float32)
            for kind in range(2):
                for side in range(4):
                    values = near_ref[table_smem[mates[turn], 2 * kind + i, side]]
                    values = pltpu.roll(values, table_smem[mates[turn], 2 * kind + i + 4, side], 2)
                    total = jnp.where(chosen[kind][side], values, total)
            pair.append(total)
        total = jnp.where((parity == 0)[None], pair[0], pair[1])
        if turn == 0:
            arriving_ref[pl.ds(chunk * here, chunk)] = total
            continue
        picked_ref[turn - 1] = total
        pltpu.make_async_remote_copy(
            src_ref=picked_ref.at[turn - 1],
            dst_ref=arriving_ref.at[pl.ds(chunk * here, chunk)],
            send_sem=send_sem.at[2],
            recv_sem=recv_sem.at[PICK_SEMS[turn]],
            device_id={"tile": own_start + mates[turn]},
            device_id_type=MESH,
        ).start()

    for members in PICK_GROUPS:
        some = arriving_ref.at[pl.ds(0, chunk * len([turn for turn in members if turn]))]
        whole(some, some, PICK_SEMS[members[-1]]).wait_recv()
        places = [chunk * mates[turn] + t for turn in members for t in range(chunk)]
        rows = [jnp.where(k < bdepth, arriving_ref[k], 0.0) for k in places]
        high, low = halves(jnp.concatenate(rows, axis=0))
        returned = jnp.dot(
            jnp.concatenate([high, low], axis=1), pla_ref[...], preferred_element_type=jnp.float32
        )
        for n, k in enumerate(places):
            result = base_ref[k] + returned[8 * n : 8 * n + 8]
            out_ref[k] = result[:, :cells]
    every = near_ref.at[pl.ds(0, 3 * PLANE - 1)]
    whole(every, every, 0).wait_send()
    told.wait_send()
    whole(picked_ref, picked_ref, 4).wait_send()


def store_kernel(held_ref, out_hbm, sem):
    for n in range(4):
        pltpu.make_async_copy(held_ref.at[:, 2 * n : 2 * n + 2], out_hbm.at[:, n], sem).start()
    pltpu.make_async_copy(out_hbm, out_hbm, sem).wait()


def shards_fast(
    cotangent,
    courant_x,
    courant_y,
    diffusivity,
    vert_diff,
    level_count,
    edge_tile,
    edge_code,
    corner_tile,
    corner_code,
):
    levels, tracers, tiles_here, cells = cotangent.shape
    count = lax.axis_size("tile")
    vmem = pl.BlockSpec(memory_space=pltpu.VMEM)
    hbm = pl.BlockSpec(memory_space=pltpu.HBM)
    chunk = levels // PLANE
    f32 = jnp.float32
    held = pl.pallas_call(
        functools.partial(exchange_kernel, count),
        name="exchange",
        out_shape=pltpu.VMEM((levels, 8, cells), f32),
        in_specs=[hbm] * 10,
        out_specs=vmem,
        scratch_shapes=[
            pltpu.VMEM((levels, 8, cells), f32),
            pltpu.VMEM((3, levels // 4, 8, cells), f32),
            pltpu.VMEM((8, cells), f32),
            pltpu.VMEM((8, cells), jnp.int32),
            pltpu.VMEM((3, levels, 8, cells), f32),
            pltpu.VMEM((4, 2, 4), jnp.int32),
            pltpu.SMEM((2, 4), jnp.int32),
            pltpu.VMEM((2 * LANES, PADDED), jnp.bfloat16),
            pltpu.VMEM((levels, 8, LANES), f32),
            pltpu.VMEM((levels // 4, 8, LANES), f32),
            pltpu.VMEM((levels, 8, LANES), f32),
            pltpu.VMEM((levels, 8, LANES), f32),
            pltpu.VMEM((levels, 8, cells), f32),
            pltpu.VMEM((levels, 8, cells), f32),
            pltpu.VMEM((levels, 8, PADDED), f32),
            pltpu.VMEM((PLANE, 8, LANES), jnp.int32),
            pltpu.SMEM((PLANE, 8, LANES), jnp.int32),
            pltpu.VMEM((2 * (3 * PLANE + 1), chunk, 8, LANES), f32),
            pltpu.VMEM((PLANE - 1, chunk, 8, LANES), f32),
            pltpu.VMEM((levels, 8, LANES), f32),
            pltpu.SemaphoreType.DMA((8,)),
            pltpu.SemaphoreType.DMA((3,)),
            pltpu.SemaphoreType.DMA((7,)),
        ],
        compiler_params=pltpu.CompilerParams(
            collective_id=0, has_side_effects=True, vmem_limit_bytes=62 << 20
        ),
    )(
        cotangent, courant_x, courant_y, diffusivity, vert_diff, level_count,
        edge_tile, edge_code, corner_tile, corner_code,
    )
    return pl.pallas_call(
        store_kernel,
        name="store",
        out_shape=jax.ShapeDtypeStruct(cotangent.shape, f32),
        in_specs=[vmem],
        out_specs=hbm,
        scratch_shapes=[pltpu.SemaphoreType.DMA],
        compiler_params=pltpu.CompilerParams(vmem_limit_bytes=8 << 20),
    )(held)


def solution(mesh):
    placed = (
        P("lev", None, "tile", None),
        P("lev", "tile", None),
        P("lev", "tile", None),
        P("tile", None),
        P("lev", "tile", None),
        P("tile", None),
        P("tile", None),
        P("tile", None),
        P("tile", None),
        P("tile", None),
    )
    fast = mesh.shape["lev"] == 1 and mesh.shape["tile"] % PLANE == 0 and mesh.shape["tile"] > 2 * BAND
    return jax.shard_map(
        shards_fast if fast else shards, mesh=mesh, in_specs=placed, out_specs=P("lev", None, "tile", None), check_vma=False
    )
```

```python
import functools

import jax
import jax.numpy as jnp
import numpy as np
from jax import lax
from jax.experimental import pallas as pl
from jax.experimental.pallas import tpu as pltpu
from jax.sharding import PartitionSpec as P

EDGE = 30
BAND = 8


stencil_offsets = [(0, -1), (0, 1), (-1, 0), (1, 0), (-1, -1), (-1, 1), (1, -1), (1, 1)]


def from_behind(value, axis, steps):
    count = lax.axis_size(axis)
    initial, last = (max(0, -steps), min(count, count - steps))
    return lax.ppermute(value, axis, [(source, source + steps) for source in range(initial, last)])


def shifted_2(value, axis, by):
    devices = lax.axis_size(axis)
    return lax.ppermute(value, axis, [(i, (i + by) % devices) for i in range(devices)])


def stencil_weights(diffuse, flow_x, flow_y):
    return [
        diffuse + 0.5 * flow_x,
        diffuse - 0.5 * flow_x,
        diffuse + 0.5 * flow_y,
        diffuse - 0.5 * flow_y,
        0.25 * diffuse,
        0.25 * diffuse,
        0.25 * diffuse,
        0.25 * diffuse,
    ]


def eliminate(right_side, coupling_up, coupling_down, initial):

    def advance(state, inputs):
        factor, partial_value = state
        source, upper_term, lower_term = inputs
        divisor = 1.0 + upper_term + lower_term + upper_term * factor
        factor_new = -lower_term / divisor
        partial_new = (source + upper_term * partial_value) / divisor
        return ((factor_new, partial_new), (factor_new, partial_new))

    final_state, outputs = lax.scan(advance, initial, (right_side, coupling_up, coupling_down))
    return outputs


def substitute(factors, partials, below_field):

    def backward(state, inputs):
        factor, partial_value = inputs
        column_value = partial_value - factor * state
        return (column_value, column_value)

    final_state, fields = lax.scan(backward, below_field, (factors, partials), reverse=True)
    return fields


def placing_table():
    cells = []
    for border in range(4):
        for position in range(EDGE):
            cells.append(
                [position, (EDGE - 1) * EDGE + position, position * EDGE, position * EDGE + EDGE - 1][border]
            )
    cells += [0, EDGE - 1, (EDGE - 1) * EDGE, EDGE * EDGE - 1]
    placing = np.zeros((len(cells), EDGE * EDGE), np.float32)
    placing[np.arange(len(cells)), np.array(cells)] = 1.0
    return placing


def embed(field):
    leading = field.shape[:-1]
    square = field.reshape(leading + (EDGE, EDGE))
    padded = jnp.pad(square, [(0, 0)] * len(leading) + [(1, 1), (1, 1)])
    return padded.reshape(leading + ((EDGE + 2) * (EDGE + 2),))


def shards(
    cotangent,
    courant_x,
    courant_y,
    diffusivity,
    vert_diff,
    level_count,
    edge_tile,
    edge_code,
    corner_tile,
    corner_code,
):
    levels_here = cotangent.shape[0]
    tracers = cotangent.shape[1]
    tiles_here = cotangent.shape[2]
    cells = cotangent.shape[3]
    padded_edge = EDGE + 2
    cycle_size = 4 * EDGE + 4
    lev_count = lax.axis_size("lev")
    depth_index = (
        lax.axis_index("lev") * levels_here
        + jnp.arange(levels_here, dtype=jnp.int32)[:, None, None]
    )
    wet_mask = (depth_index < level_count[None]).astype(jnp.float32)
    coupling = jnp.where(depth_index == 0, jnp.float32(0.0), vert_diff * wet_mask)
    deeper = from_behind(coupling[0], "lev", -1)
    coupling_down = jnp.concatenate([coupling[1:], deeper[None]], axis=0)[:, None]
    coupling_up = coupling[:, None]
    initial = (
        jnp.zeros((1, tiles_here, cells), jnp.float32),
        jnp.zeros((tracers, tiles_here, cells), jnp.float32),
    )
    for sweep_index in range(lev_count - 1):
        factors, partials = eliminate(cotangent, coupling_up, coupling_down, initial)
        initial = from_behind((factors[-1], partials[-1]), "lev", 1)
    factors, partials = eliminate(cotangent, coupling_up, coupling_down, initial)
    below_field = jnp.zeros((tracers, tiles_here, cells), jnp.float32)
    for sweep_index in range(lev_count - 1):
        fields = substitute(factors, partials, below_field)
        below_field = from_behind(fields[0], "lev", -1)
    solved = substitute(factors, partials, below_field)
    weighted = solved * wet_mask[:, None]
    weighted_ext = embed(weighted)
    diffuse_ext = embed(diffusivity)[None, None]
    flow_x_ext = embed(courant_x)[:, None]
    flow_y_ext = embed(courant_y)[:, None]
    weights = stencil_weights(diffuse_ext, flow_x_ext, flow_y_ext)
    leading = weighted_ext.shape[:-1]
    spread = jnp.zeros_like(weighted_ext)
    for (shift_row, shift_col), weight in zip(stencil_offsets, weights):
        contribution = weight * weighted_ext
        offset = shift_row * padded_edge + shift_col
        if offset > 0:
            shifted = jnp.concatenate(
                [jnp.zeros(leading + (offset,), jnp.float32), contribution[..., :-offset]], axis=-1
            )
        else:
            shifted = jnp.concatenate(
                [contribution[..., -offset:], jnp.zeros(leading + (-offset,), jnp.float32)], axis=-1
            )
        spread = spread + shifted
    placing = placing_table()
    framed = spread.reshape(leading + (padded_edge, padded_edge))
    outgoing = jnp.concatenate(
        [
            framed[..., 0, 1:-1],
            framed[..., -1, 1:-1],
            framed[..., 1:-1, 0],
            framed[..., 1:-1, -1],
            framed[..., 0, :1],
            framed[..., 0, -1:],
            framed[..., -1, :1],
            framed[..., -1, -1:],
        ],
        axis=-1,
    )
    interior = spread.reshape(leading + (padded_edge, padded_edge))[..., 1:-1, 1:-1].reshape(
        solved.shape
    )
    partners = jnp.concatenate([edge_tile, corner_tile], axis=1)

    def collect(gathered_sum, portion, first_tile):
        tile_span = portion.shape[2]
        onehot = (
            partners[:, :, None]
            == first_tile + jnp.arange(tile_span, dtype=jnp.int32)[None, None, :]
        ).astype(jnp.float32)
        return gathered_sum + jnp.einsum(
            "tkw,dnwr->dntkr", onehot, portion, precision=lax.Precision.HIGHEST
        )

    tile_count = lax.axis_size("tile")
    own_index = lax.axis_index("tile")
    reach = (2 * BAND + tiles_here - 1) // tiles_here
    fetched = collect(
        jnp.zeros((levels_here, tracers, tiles_here, 8, cycle_size), jnp.float32),
        outgoing,
        own_index * tiles_here,
    )
    for distance in range(-reach, reach + 1):
        if distance != 0:
            portion = shifted_2(outgoing, "tile", distance)
            source = (own_index - distance) % tile_count
            fetched = collect(fetched, portion, source * tiles_here)
    side_values = fetched[:, :, :, :4, : 4 * EDGE].reshape(
        levels_here, tracers, tiles_here, 4, 4, EDGE
    )
    side_choice = (
        (edge_code % 4)[:, :, None] == jnp.arange(4, dtype=jnp.int32)[None, None, :]
    ).astype(jnp.float32)
    strips = jnp.sum(side_values * side_choice[None, None, :, :, :, None], axis=4)
    strips = jnp.where((edge_code >= 4)[None, None, :, :, None], strips[..., ::-1], strips)
    corner_values = fetched[:, :, :, 4:, 4 * EDGE :]
    corner_choice = (
        corner_code[:, :, None] == jnp.arange(4, dtype=jnp.int32)[None, None, :]
    ).astype(jnp.float32)
    corner_picked = jnp.sum(corner_values * corner_choice[None, None], axis=4)
    arriving = jnp.concatenate(
        [strips.reshape(levels_here, tracers, tiles_here, 4 * EDGE), corner_picked], axis=3
    )
    returned = jnp.einsum(
        "dntr,rc->dntc", arriving, jnp.asarray(placing), precision=lax.Precision.HIGHEST
    )
    diffuse_here = diffusivity[None, None]
    return wet_mask[:, None] * ((1.0 - 5.0 * diffuse_here) * weighted + interior + returned)


PADDED = 1024
LANES = 128
GROUP = 32
PLANE = 8
MESH = pl.DeviceIdType.MESH
SEND_SEMS = (0, 0, 0, 1, 2, 2, 2)
PICK_SEMS = {1: 4, 3: 5, 2: 5, 5: 5, 4: 5, 7: 6, 6: 6}
PICK_GROUPS = [(0, 1), (3, 2, 5, 4), (7, 6)]


def cell_of(lane):
    group, spot = lane // GROUP, lane & (GROUP - 1)
    along = jnp.where(spot < EDGE, spot, 0)
    cell = jnp.where(group == 0, along, (EDGE - 1) * EDGE + along)
    cell = jnp.where(group == 2, EDGE * along, cell)
    cell = jnp.where(group == 3, EDGE * along + EDGE - 1, cell)
    corner = jnp.where(group >= 2, (EDGE - 1) * EDGE, 0) + jnp.where((group & 1) == 1, EDGE - 1, 0)
    return jnp.where(spot < EDGE, cell, jnp.where(spot == EDGE, corner, -1))


def halves(value):
    high = value.astype(jnp.bfloat16)
    return high, (value - high.astype(jnp.float32)).astype(jnp.bfloat16)


def widen(rows):
    return jnp.concatenate(
        [rows, jnp.zeros((rows.shape[0], PADDED - rows.shape[1]), rows.dtype)], axis=1
    )


def exchange_kernel(
    count,
    cot_hbm, cx_hbm, cy_hbm, dif_hbm, vd_hbm, lc_hbm, et_hbm, ec_hbm, ct_hbm, cc_hbm,
    out_ref,
    cot_ref, quads_ref, dif_ref, lc_ref, wide_ref,
    lists_ref, code_ref, pla_ref,
    bcot_ref, bvd_ref, bflow_ref, strips_ref, factor_ref, partial_ref, base_ref,
    tables_ref, table_smem, near_ref, picked_ref, arriving_ref,
    in_sem, send_sem, recv_sem,
):
    levels = cot_ref.shape[0]
    quad = levels // 4
    chunk = levels // PLANE
    cells = cot_ref.shape[2]
    planes = count // PLANE
    slots = 3 * PLANE + 1
    me = lax.axis_index("tile")
    plane = me // PLANE
    here = lax.rem(me, PLANE)

    def start_of(step):
        return PLANE * lax.rem(plane + step + planes, planes)

    mates = [here ^ turn for turn in range(PLANE)]
    own_start = PLANE * plane

    low_end = (planes - plane) // planes
    second_plane = (planes + 1 - plane) // planes * (1 - low_end)
    leap = 1 - 2 * second_plane
    leap_start, other_start = start_of(leap), start_of(-leap)
    turns = [6, 7, 4, 5, 2, 3, 1, 0]

    barrier = pltpu.get_barrier_semaphore()
    peers = [own_start + mates[turn] for turn in turns if turn]
    peers += [start + mates[turn] for start in (leap_start, other_start) for turn in turns]
    for peer in peers:
        pl.semaphore_signal(barrier, inc=1, device_id={"tile": peer}, device_id_type=MESH)

    used = []

    def fetch(pairs, whole):
        sem = in_sem.at[len(used)]
        used.append(whole)
        for source, target in pairs:
            pltpu.make_async_copy(source, target, sem).start()
        return pltpu.make_async_copy(whole, whole, sem)

    def fetch_flat(source, target):
        return fetch([(source, target.at[2 * n : 2 * n + 2]) for n in range(4)], target)

    columns = [vd_hbm, cx_hbm, cy_hbm]
    first = [
        fetch(
            [
                (source.at[quad * j : quad * j + quad], quads_ref.at[i, :, 2 * j : 2 * j + 2])
                for i, source in enumerate(columns)
                for j in range(4)
            ],
            quads_ref,
        ),
        fetch_flat(lc_hbm, lc_ref),
    ]
    second = fetch([(cot_hbm.at[:, n], cot_ref.at[:, 2 * n : 2 * n + 2]) for n in range(4)], cot_ref)
    first += [fetch_flat(dif_hbm, dif_ref), fetch([(ec_hbm, code_ref)], code_ref)]
    lists = fetch(
        [(source, lists_ref.at[i]) for i, source in enumerate([et_hbm, ec_hbm, ct_hbm, cc_hbm])],
        lists_ref,
    )
    lane = lax.broadcasted_iota(jnp.int32, (8, LANES), 1)
    row = lax.broadcasted_iota(jnp.int32, (8, LANES), 0)
    parity = row & 1
    group = lane // GROUP
    spot = lane & (GROUP - 1)
    on_side = spot < EDGE

    cells_at = cell_of(lane)
    block_of, lane_of = jnp.where(cells_at < 0, -1, cells_at // LANES), cells_at & (LANES - 1)

    def gather(rows):
        groups = []
        for g in range(rows.shape[0] // 8):
            some = widen(rows[8 * g : 8 * g + 8])
            total = jnp.zeros((8, LANES), rows.dtype)
            for b in range(PADDED // LANES):
                block = jnp.take_along_axis(some[:, LANES * b : LANES * b + LANES], lane_of, axis=1)
                total = jnp.where(block_of == b, block, total)
            groups.append(total)
        return jnp.concatenate(groups, axis=0)

    def spread_rows(values, j):
        return jnp.take_along_axis(values, 2 * j + parity, axis=0)

    for copy in first:
        copy.wait()
    bdepth = gather(lc_ref[...])
    bvd_ref[...] = gather(quads_ref[0].reshape(8 * quad, cells)).reshape(quad, 8, LANES)

    def bcoupling(k):
        if k == 0 or k == levels:
            return jnp.zeros((8, LANES), jnp.float32)
        return jnp.where(k < bdepth, spread_rows(bvd_ref[k % quad], k // quad), 0.0)

    bdif = gather(dif_ref[...])
    along = gather(quads_ref[1].reshape(8 * quad, cells)).reshape(quad, 8, LANES)
    across = gather(quads_ref[2].reshape(8 * quad, cells)).reshape(quad, 8, LANES)
    quarter = 0.25 * bdif
    weight = jnp.where(on_side, bdif, quarter)
    for g in range(quad):
        flow = 0.5 * jnp.where(group < 2, across[g], along[g])
        flow = jnp.where(on_side, jnp.where((group & 1) == 0, flow, -flow), 0.0)
        for j in range(4):
            bflow_ref[quad * j + g] = weight + spread_rows(flow, j)
    code = jnp.zeros((8, LANES), jnp.int32)
    for i in range(2):
        for side in range(4):
            code = jnp.where((parity == i) & (group == side), code_ref[i, side], code)
    turned = jnp.where((code >= 4) & on_side, GROUP * group + (EDGE - 1) - spot, lane)

    middle = levels // 2
    zero = jnp.zeros((8, LANES), jnp.float32)
    coupled = [bcoupling(k) for k in range(levels + 1)]
    inverse, link = [None] * levels, [None] * levels
    excess, low_excess = zero + 1.0, zero + 1.0
    for k in range(middle):
        m = levels - 1 - k
        total, low_total = coupled[k + 1] + excess, coupled[m] + low_excess
        if k < middle - 1:
            inverse[k], inverse[m] = 1.0 / total, 1.0 / low_total
            link[k], link[m] = coupled[k + 1] * inverse[k], coupled[m] * inverse[m]
            excess, low_excess = 1.0 + link[k] * excess, 1.0 + link[m] * low_excess
    joint = coupled[middle]
    meeting = 1.0 / (joint * (excess + low_excess) + excess * low_excess)

    second.wait()
    bcot_ref[...] = gather(cot_ref[...].reshape(8 * levels, cells)).reshape(levels, 8, LANES)
    wide = fetch(
        [
            (source, wide_ref.at[i, :, 2 * n : 2 * n + 2])
            for i, source in enumerate(columns)
            for n in range(4)
        ],
        wide_ref,
    )
    value = [None] * levels
    part, low_part = zero, zero
    for k in range(middle):
        m = levels - 1 - k
        source = bcot_ref[k] + coupled[k] * part
        low_source = bcot_ref[m] + coupled[m + 1] * low_part
        if k < middle - 1:
            part, low_part = source * inverse[k], low_source * inverse[m]
            value[k], value[m] = part, low_part
    value[middle] = (low_source * total + joint * source) * meeting
    value[middle - 1] = (source * low_total + joint * low_source) * meeting
    for k in range(middle - 2, -1, -1):
        m = levels - 1 - k
        value[k] = value[k] + link[k] * value[k + 1]
        value[m] = value[m] + link[m] * value[m - 1]
    for k in range(levels):
        u = jnp.where(k < bdepth, value[k], 0.0)
        diagonal = jnp.where(on_side, quarter * u, 0.0)
        beside = pltpu.roll(diagonal, 1, 1) + pltpu.roll(diagonal, LANES - 1, 1)
        halo = bflow_ref[k] * u + jnp.where(on_side, beside, 0.0)
        strips_ref[k] = jnp.take_along_axis(halo, turned, axis=1)

    lists.wait()
    tile_index = lax.broadcasted_iota(jnp.int32, (2, 4), 0)
    side_index = lax.broadcasted_iota(jnp.int32, (2, 4), 1)
    tables_ref[here] = jnp.zeros((8, LANES), jnp.int32)
    for part_index in range(2):
        tile, kind = lists_ref[2 * part_index], lists_ref[2 * part_index + 1]
        device = tile >> 1
        step = device // PLANE - plane + 1
        step = jnp.where(step < 0, step + planes, step)
        step = jnp.where(step >= planes, step - planes, step)
        slot = PLANE * step + (device & (PLANE - 1))
        slot = jnp.where((tile < 0) | (step > 2), 3 * PLANE, slot)
        swapped = (tile & 1) ^ tile_index
        shift = GROUP * ((side_index - (kind & 3)) & 3)
        tables_ref[here, 2 * part_index : 2 * part_index + 2, 0:4] = slots * swapped + slot
        tables_ref[here, 2 * part_index + 4 : 2 * part_index + 6, 0:4] = shift

    pl.semaphore_wait(barrier, len(peers))

    def send(step, start, some):
        mark = PLANE * (1 - step) + here
        for turn in some:
            pltpu.make_async_remote_copy(
                src_ref=strips_ref.at[pl.ds(chunk * mates[turn], chunk)],
                dst_ref=near_ref.at[mark],
                send_sem=send_sem.at[0],
                recv_sem=recv_sem.at[1 - step],
                device_id={"tile": start + mates[turn]},
                device_id_type=MESH,
            ).start()

    def whole(source, target, mark):
        return pltpu.make_async_remote_copy(
            src_ref=source,
            dst_ref=target,
            send_sem=send_sem.at[SEND_SEMS[mark]],
            recv_sem=recv_sem.at[mark],
            device_id={"tile": own_start + mates[1]},
            device_id_type=MESH,
        )

    @pl.when(low_end == 1)
    def _():
        send(0, own_start, turns[:-1])
        send(leap, leap_start, turns)
        send(-leap, other_start, turns)

    @pl.when(low_end == 0)
    def _():
        send(leap, leap_start, turns)
        send(0, own_start, turns[:-1])
        send(-leap, other_start, turns)

    for turn in turns[:-1]:
        pltpu.make_async_remote_copy(
            src_ref=tables_ref.at[here],
            dst_ref=tables_ref.at[here],
            send_sem=send_sem.at[1],
            recv_sem=recv_sem.at[3],
            device_id={"tile": own_start + mates[turn]},
            device_id_type=MESH,
        ).start()
    near_ref[PLANE + here] = strips_ref[pl.ds(chunk * here, chunk)]
    for slot in (slots - 1, 2 * slots - 1):
        near_ref[slot] = jnp.zeros((chunk, 8, LANES), jnp.float32)

    spots = lax.broadcasted_iota(jnp.int32, (LANES, PADDED), 1)
    cells_at = cell_of(lax.broadcasted_iota(jnp.int32, (LANES, 1), 0))
    placer = jnp.where(spots == cells_at, 1.0, 0.0).astype(jnp.bfloat16)
    pla_ref[0:LANES] = placer
    pla_ref[LANES:] = placer
    wide.wait()
    depth = lc_ref[...]

    def advance(k, state):
        up, excess, part = state
        later = jnp.minimum(k + 1, levels - 1)
        down = jnp.where(k + 1 < depth, wide_ref[0, later], 0.0)
        down = jnp.where(k + 1 < levels, down, 0.0)
        inverse = 1.0 / (down + excess)
        factor = down * inverse
        part = (cot_ref[k] + up * part) * inverse
        factor_ref[k] = factor
        partial_ref[k] = part
        return down, 1.0 + factor * excess, part

    blank = jnp.zeros((8, cells), jnp.float32)
    lax.fori_loop(0, levels, advance, (blank, blank + 1.0, blank), unroll=2)

    wide_lane = lax.broadcasted_iota(jnp.int32, (8, PADDED), 1)
    wraps = PADDED - EDGE
    column = lax.rem(jnp.where(wide_lane >= wraps, wide_lane - wraps, wide_lane), EDGE)
    not_first = column != 0
    not_last = column != EDGE - 1
    diffuse = widen(dif_ref[...])
    quarter_wide = 0.25 * diffuse
    centre = 1.0 - 5.0 * diffuse
    wide_depth = widen(depth)

    def substitute_back(step, solved):
        k = levels - 1 - step
        solved = partial_ref[k] + factor_ref[k] * solved
        u = widen(jnp.where(k < depth, solved, 0.0))
        half_x = 0.5 * widen(wide_ref[1, k])
        half_y = 0.5 * widen(wide_ref[2, k])
        diagonal = quarter_wide * u
        both = pltpu.roll(diagonal, EDGE, 1) + pltpu.roll(diagonal, PADDED - EDGE, 1)
        west = both + (diffuse + half_x) * u
        east = both + (diffuse - half_x) * u
        total = pltpu.roll((diffuse + half_y) * u, PADDED - EDGE, 1)
        total = total + pltpu.roll((diffuse - half_y) * u, EDGE, 1)
        total = total + pltpu.roll(jnp.where(not_first, west, 0.0), PADDED - 1, 1)
        total = total + pltpu.roll(jnp.where(not_last, east, 0.0), 1, 1)
        base_ref[k] = jnp.where(k < wide_depth, centre * u + total, 0.0)
        return solved

    lax.fori_loop(0, levels, substitute_back, blank, unroll=2)

    others = pl.ds(0, PLANE - 1)
    told = whole(tables_ref.at[others], tables_ref.at[others], 3)
    told.wait_recv()
    to_smem = pltpu.make_async_copy(tables_ref, table_smem, in_sem.at[len(used)])
    to_smem.start()

    for below in (1, 2, 0):
        group_slots = PLANE - 1 if below == 1 else PLANE
        some = near_ref.at[pl.ds(PLANE * below, group_slots)]
        whole(some, some, below).wait_recv()
        for slot in range(PLANE * below, PLANE * below + PLANE):
            for t in range(chunk):
                near_ref[slots + slot, t] = jnp.take_along_axis(near_ref[slot, t], row ^ 1, axis=0)
    to_smem.wait()

    chosen = [[(wanted & (group == side))[None] for side in range(4)] for wanted in (on_side, spot == EDGE)]
    for turn in turns:
        pair = []
        for i in range(2):
            total = jnp.zeros((chunk, 8, LANES), jnp.float32)
            for kind in range(2):
                for side in range(4):
                    values = near_ref[table_smem[mates[turn], 2 * kind + i, side]]
                    values = pltpu.roll(values, table_smem[mates[turn], 2 * kind + i + 4, side], 2)
                    total = jnp.where(chosen[kind][side], values, total)
            pair.append(total)
        total = jnp.where((parity == 0)[None], pair[0], pair[1])
        if turn == 0:
            arriving_ref[pl.ds(chunk * here, chunk)] = total
            continue
        picked_ref[turn - 1] = total
        pltpu.make_async_remote_copy(
            src_ref=picked_ref.at[turn - 1],
            dst_ref=arriving_ref.at[pl.ds(chunk * here, chunk)],
            send_sem=send_sem.at[2],
            recv_sem=recv_sem.at[PICK_SEMS[turn]],
            device_id={"tile": own_start + mates[turn]},
            device_id_type=MESH,
        ).start()

    for members in PICK_GROUPS:
        some = arriving_ref.at[pl.ds(0, chunk * len([turn for turn in members if turn]))]
        whole(some, some, PICK_SEMS[members[-1]]).wait_recv()
        places = [chunk * mates[turn] + t for turn in members for t in range(chunk)]
        rows = [jnp.where(k < bdepth, arriving_ref[k], 0.0) for k in places]
        high, low = halves(jnp.concatenate(rows, axis=0))
        returned = jnp.dot(
            jnp.concatenate([high, low], axis=1), pla_ref[...], preferred_element_type=jnp.float32
        )
        for n, k in enumerate(places):
            result = base_ref[k] + returned[8 * n : 8 * n + 8]
            out_ref[k] = result[:, :cells]
    every = near_ref.at[pl.ds(0, 3 * PLANE - 1)]
    whole(every, every, 0).wait_send()
    told.wait_send()
    whole(picked_ref, picked_ref, 4).wait_send()


def store_kernel(held_ref, out_hbm, sem):
    for n in range(4):
        pltpu.make_async_copy(held_ref.at[:, 2 * n : 2 * n + 2], out_hbm.at[:, n], sem).start()
    pltpu.make_async_copy(out_hbm, out_hbm, sem).wait()


def shards_fast(
    cotangent,
    courant_x,
    courant_y,
    diffusivity,
    vert_diff,
    level_count,
    edge_tile,
    edge_code,
    corner_tile,
    corner_code,
):
    levels, tracers, tiles_here, cells = cotangent.shape
    count = lax.axis_size("tile")
    vmem = pl.BlockSpec(memory_space=pltpu.VMEM)
    hbm = pl.BlockSpec(memory_space=pltpu.HBM)
    chunk = levels // PLANE
    f32 = jnp.float32
    held = pl.pallas_call(
        functools.partial(exchange_kernel, count),
        name="exchange",
        out_shape=pltpu.VMEM((levels, 8, cells), f32),
        in_specs=[hbm] * 10,
        out_specs=vmem,
        scratch_shapes=[
            pltpu.VMEM((levels, 8, cells), f32),
            pltpu.VMEM((3, levels // 4, 8, cells), f32),
            pltpu.VMEM((8, cells), f32),
            pltpu.VMEM((8, cells), jnp.int32),
            pltpu.VMEM((3, levels, 8, cells), f32),
            pltpu.VMEM((4, 2, 4), jnp.int32),
            pltpu.SMEM((2, 4), jnp.int32),
            pltpu.VMEM((2 * LANES, PADDED), jnp.bfloat16),
            pltpu.VMEM((levels, 8, LANES), f32),
            pltpu.VMEM((levels // 4, 8, LANES), f32),
            pltpu.VMEM((levels, 8, LANES), f32),
            pltpu.VMEM((levels, 8, LANES), f32),
            pltpu.VMEM((levels, 8, cells), f32),
            pltpu.VMEM((levels, 8, cells), f32),
            pltpu.VMEM((levels, 8, PADDED), f32),
            pltpu.VMEM((PLANE, 8, LANES), jnp.int32),
            pltpu.SMEM((PLANE, 8, LANES), jnp.int32),
            pltpu.VMEM((2 * (3 * PLANE + 1), chunk, 8, LANES), f32),
            pltpu.VMEM((PLANE - 1, chunk, 8, LANES), f32),
            pltpu.VMEM((levels, 8, LANES), f32),
            pltpu.SemaphoreType.DMA((8,)),
            pltpu.SemaphoreType.DMA((3,)),
            pltpu.SemaphoreType.DMA((7,)),
        ],
        compiler_params=pltpu.CompilerParams(
            collective_id=0, has_side_effects=True, vmem_limit_bytes=62 << 20
        ),
    )(
        cotangent, courant_x, courant_y, diffusivity, vert_diff, level_count,
        edge_tile, edge_code, corner_tile, corner_code,
    )
    return pl.pallas_call(
        store_kernel,
        name="store",
        out_shape=jax.ShapeDtypeStruct(cotangent.shape, f32),
        in_specs=[vmem],
        out_specs=hbm,
        scratch_shapes=[pltpu.SemaphoreType.DMA],
        compiler_params=pltpu.CompilerParams(vmem_limit_bytes=8 << 20),
    )(held)


def solution(mesh):
    placed = (
        P("lev", None, "tile", None),
        P("lev", "tile", None),
        P("lev", "tile", None),
        P("tile", None),
        P("lev", "tile", None),
        P("tile", None),
        P("tile", None),
        P("tile", None),
        P("tile", None),
        P("tile", None),
    )
    fast = mesh.shape["lev"] == 1 and mesh.shape["tile"] % PLANE == 0 and mesh.shape["tile"] > 2 * BAND
    return jax.shard_map(
        shards_fast if fast else shards, mesh=mesh, in_specs=placed, out_specs=P("lev", None, "tile", None), check_vma=False
    )
```

```python
import functools

import jax
import jax.numpy as jnp
import numpy as np
from jax import lax
from jax.experimental import pallas as pl
from jax.experimental.pallas import tpu as pltpu
from jax.sharding import PartitionSpec as P

EDGE = 30
BAND = 8


stencil_offsets = [(0, -1), (0, 1), (-1, 0), (1, 0), (-1, -1), (-1, 1), (1, -1), (1, 1)]


def from_behind(value, axis, steps):
    count = lax.axis_size(axis)
    initial, last = (max(0, -steps), min(count, count - steps))
    return lax.ppermute(value, axis, [(source, source + steps) for source in range(initial, last)])


def shifted_2(value, axis, by):
    devices = lax.axis_size(axis)
    return lax.ppermute(value, axis, [(i, (i + by) % devices) for i in range(devices)])


def stencil_weights(diffuse, flow_x, flow_y):
    return [
        diffuse + 0.5 * flow_x,
        diffuse - 0.5 * flow_x,
        diffuse + 0.5 * flow_y,
        diffuse - 0.5 * flow_y,
        0.25 * diffuse,
        0.25 * diffuse,
        0.25 * diffuse,
        0.25 * diffuse,
    ]


def eliminate(right_side, coupling_up, coupling_down, initial):

    def advance(state, inputs):
        factor, partial_value = state
        source, upper_term, lower_term = inputs
        divisor = 1.0 + upper_term + lower_term + upper_term * factor
        factor_new = -lower_term / divisor
        partial_new = (source + upper_term * partial_value) / divisor
        return ((factor_new, partial_new), (factor_new, partial_new))

    final_state, outputs = lax.scan(advance, initial, (right_side, coupling_up, coupling_down))
    return outputs


def substitute(factors, partials, below_field):

    def backward(state, inputs):
        factor, partial_value = inputs
        column_value = partial_value - factor * state
        return (column_value, column_value)

    final_state, fields = lax.scan(backward, below_field, (factors, partials), reverse=True)
    return fields


def placing_table():
    cells = []
    for border in range(4):
        for position in range(EDGE):
            cells.append(
                [position, (EDGE - 1) * EDGE + position, position * EDGE, position * EDGE + EDGE - 1][border]
            )
    cells += [0, EDGE - 1, (EDGE - 1) * EDGE, EDGE * EDGE - 1]
    placing = np.zeros((len(cells), EDGE * EDGE), np.float32)
    placing[np.arange(len(cells)), np.array(cells)] = 1.0
    return placing


def embed(field):
    leading = field.shape[:-1]
    square = field.reshape(leading + (EDGE, EDGE))
    padded = jnp.pad(square, [(0, 0)] * len(leading) + [(1, 1), (1, 1)])
    return padded.reshape(leading + ((EDGE + 2) * (EDGE + 2),))


def shards(
    cotangent,
    courant_x,
    courant_y,
    diffusivity,
    vert_diff,
    level_count,
    edge_tile,
    edge_code,
    corner_tile,
    corner_code,
):
    levels_here = cotangent.shape[0]
    tracers = cotangent.shape[1]
    tiles_here = cotangent.shape[2]
    cells = cotangent.shape[3]
    padded_edge = EDGE + 2
    cycle_size = 4 * EDGE + 4
    lev_count = lax.axis_size("lev")
    depth_index = (
        lax.axis_index("lev") * levels_here
        + jnp.arange(levels_here, dtype=jnp.int32)[:, None, None]
    )
    wet_mask = (depth_index < level_count[None]).astype(jnp.float32)
    coupling = jnp.where(depth_index == 0, jnp.float32(0.0), vert_diff * wet_mask)
    deeper = from_behind(coupling[0], "lev", -1)
    coupling_down = jnp.concatenate([coupling[1:], deeper[None]], axis=0)[:, None]
    coupling_up = coupling[:, None]
    initial = (
        jnp.zeros((1, tiles_here, cells), jnp.float32),
        jnp.zeros((tracers, tiles_here, cells), jnp.float32),
    )
    for sweep_index in range(lev_count - 1):
        factors, partials = eliminate(cotangent, coupling_up, coupling_down, initial)
        initial = from_behind((factors[-1], partials[-1]), "lev", 1)
    factors, partials = eliminate(cotangent, coupling_up, coupling_down, initial)
    below_field = jnp.zeros((tracers, tiles_here, cells), jnp.float32)
    for sweep_index in range(lev_count - 1):
        fields = substitute(factors, partials, below_field)
        below_field = from_behind(fields[0], "lev", -1)
    solved = substitute(factors, partials, below_field)
    weighted = solved * wet_mask[:, None]
    weighted_ext = embed(weighted)
    diffuse_ext = embed(diffusivity)[None, None]
    flow_x_ext = embed(courant_x)[:, None]
    flow_y_ext = embed(courant_y)[:, None]
    weights = stencil_weights(diffuse_ext, flow_x_ext, flow_y_ext)
    leading = weighted_ext.shape[:-1]
    spread = jnp.zeros_like(weighted_ext)
    for (shift_row, shift_col), weight in zip(stencil_offsets, weights):
        contribution = weight * weighted_ext
        offset = shift_row * padded_edge + shift_col
        if offset > 0:
            shifted = jnp.concatenate(
                [jnp.zeros(leading + (offset,), jnp.float32), contribution[..., :-offset]], axis=-1
            )
        else:
            shifted = jnp.concatenate(
                [contribution[..., -offset:], jnp.zeros(leading + (-offset,), jnp.float32)], axis=-1
            )
        spread = spread + shifted
    placing = placing_table()
    framed = spread.reshape(leading + (padded_edge, padded_edge))
    outgoing = jnp.concatenate(
        [
            framed[..., 0, 1:-1],
            framed[..., -1, 1:-1],
            framed[..., 1:-1, 0],
            framed[..., 1:-1, -1],
            framed[..., 0, :1],
            framed[..., 0, -1:],
            framed[..., -1, :1],
            framed[..., -1, -1:],
        ],
        axis=-1,
    )
    interior = spread.reshape(leading + (padded_edge, padded_edge))[..., 1:-1, 1:-1].reshape(
        solved.shape
    )
    partners = jnp.concatenate([edge_tile, corner_tile], axis=1)

    def collect(gathered_sum, portion, first_tile):
        tile_span = portion.shape[2]
        onehot = (
            partners[:, :, None]
            == first_tile + jnp.arange(tile_span, dtype=jnp.int32)[None, None, :]
        ).astype(jnp.float32)
        return gathered_sum + jnp.einsum(
            "tkw,dnwr->dntkr", onehot, portion, precision=lax.Precision.HIGHEST
        )

    tile_count = lax.axis_size("tile")
    own_index = lax.axis_index("tile")
    reach = (2 * BAND + tiles_here - 1) // tiles_here
    fetched = collect(
        jnp.zeros((levels_here, tracers, tiles_here, 8, cycle_size), jnp.float32),
        outgoing,
        own_index * tiles_here,
    )
    for distance in range(-reach, reach + 1):
        if distance != 0:
            portion = shifted_2(outgoing, "tile", distance)
            source = (own_index - distance) % tile_count
            fetched = collect(fetched, portion, source * tiles_here)
    side_values = fetched[:, :, :, :4, : 4 * EDGE].reshape(
        levels_here, tracers, tiles_here, 4, 4, EDGE
    )
    side_choice = (
        (edge_code % 4)[:, :, None] == jnp.arange(4, dtype=jnp.int32)[None, None, :]
    ).astype(jnp.float32)
    strips = jnp.sum(side_values * side_choice[None, None, :, :, :, None], axis=4)
    strips = jnp.where((edge_code >= 4)[None, None, :, :, None], strips[..., ::-1], strips)
    corner_values = fetched[:, :, :, 4:, 4 * EDGE :]
    corner_choice = (
        corner_code[:, :, None] == jnp.arange(4, dtype=jnp.int32)[None, None, :]
    ).astype(jnp.float32)
    corner_picked = jnp.sum(corner_values * corner_choice[None, None], axis=4)
    arriving = jnp.concatenate(
        [strips.reshape(levels_here, tracers, tiles_here, 4 * EDGE), corner_picked], axis=3
    )
    returned = jnp.einsum(
        "dntr,rc->dntc", arriving, jnp.asarray(placing), precision=lax.Precision.HIGHEST
    )
    diffuse_here = diffusivity[None, None]
    return wet_mask[:, None] * ((1.0 - 5.0 * diffuse_here) * weighted + interior + returned)


PADDED = 1024
LANES = 128
GROUP = 32
PLANE = 8
MESH = pl.DeviceIdType.MESH
SEND_SEMS = (0, 0, 0, 1, 2, 2, 2)
PICK_SEMS = {1: 4, 3: 5, 2: 5, 5: 5, 4: 5, 7: 6, 6: 6}
PICK_GROUPS = [(0, 1), (3, 2, 5, 4), (7, 6)]


def cell_of(lane):
    group, spot = lane // GROUP, lane & (GROUP - 1)
    along = jnp.where(spot < EDGE, spot, 0)
    cell = jnp.where(group == 0, along, (EDGE - 1) * EDGE + along)
    cell = jnp.where(group == 2, EDGE * along, cell)
    cell = jnp.where(group == 3, EDGE * along + EDGE - 1, cell)
    corner = jnp.where(group >= 2, (EDGE - 1) * EDGE, 0) + jnp.where((group & 1) == 1, EDGE - 1, 0)
    return jnp.where(spot < EDGE, cell, jnp.where(spot == EDGE, corner, -1))


def halves(value):
    high = value.astype(jnp.bfloat16)
    return high, (value - high.astype(jnp.float32)).astype(jnp.bfloat16)


def widen(rows):
    return jnp.concatenate(
        [rows, jnp.zeros((rows.shape[0], PADDED - rows.shape[1]), rows.dtype)], axis=1
    )


def exchange_kernel(
    count,
    cot_hbm, cx_hbm, cy_hbm, dif_hbm, vd_hbm, lc_hbm, et_hbm, ec_hbm, ct_hbm, cc_hbm,
    out_ref,
    cot_ref, quads_ref, dif_ref, lc_ref, wide_ref,
    lists_ref, code_ref, pla_ref,
    bcot_ref, bvd_ref, bflow_ref, strips_ref, factor_ref, partial_ref, base_ref,
    tables_ref, table_smem, near_ref, picked_ref, arriving_ref,
    in_sem, send_sem, recv_sem,
):
    levels = cot_ref.shape[0]
    quad = levels // 4
    chunk = levels // PLANE
    cells = cot_ref.shape[2]
    planes = count // PLANE
    slots = 3 * PLANE + 1
    me = lax.axis_index("tile")
    plane = me // PLANE
    here = lax.rem(me, PLANE)

    def start_of(step):
        return PLANE * lax.rem(plane + step + planes, planes)

    mates = [here ^ turn for turn in range(PLANE)]
    own_start = PLANE * plane

    low_end = (planes - plane) // planes
    second_plane = (planes + 1 - plane) // planes * (1 - low_end)
    leap = 1 - 2 * second_plane
    leap_start, other_start = start_of(leap), start_of(-leap)
    turns = [6, 7, 4, 5, 2, 3, 1, 0]

    barrier = pltpu.get_barrier_semaphore()
    peers = [start + mates[turn] for start in (leap_start, other_start) for turn in turns]
    peers += [own_start + mates[turn] for turn in turns if turn]
    for peer in peers:
        pl.semaphore_signal(barrier, inc=1, device_id={"tile": peer}, device_id_type=MESH)

    used = []

    def fetch(pairs, whole):
        sem = in_sem.at[len(used)]
        used.append(whole)
        for source, target in pairs:
            pltpu.make_async_copy(source, target, sem).start()
        return pltpu.make_async_copy(whole, whole, sem)

    def fetch_flat(source, target):
        return fetch([(source, target.at[2 * n : 2 * n + 2]) for n in range(4)], target)

    columns = [vd_hbm, cx_hbm, cy_hbm]
    first = [
        fetch(
            [
                (source.at[quad * j : quad * j + quad], quads_ref.at[i, :, 2 * j : 2 * j + 2])
                for i, source in enumerate(columns)
                for j in range(4)
            ],
            quads_ref,
        ),
        fetch_flat(lc_hbm, lc_ref),
    ]
    second = fetch([(cot_hbm.at[:, n], cot_ref.at[:, 2 * n : 2 * n + 2]) for n in range(4)], cot_ref)
    first += [fetch_flat(dif_hbm, dif_ref), fetch([(ec_hbm, code_ref)], code_ref)]
    lists = fetch(
        [(source, lists_ref.at[i]) for i, source in enumerate([et_hbm, ec_hbm, ct_hbm, cc_hbm])],
        lists_ref,
    )
    lane = lax.broadcasted_iota(jnp.int32, (8, LANES), 1)
    row = lax.broadcasted_iota(jnp.int32, (8, LANES), 0)
    parity = row & 1
    group = lane // GROUP
    spot = lane & (GROUP - 1)
    on_side = spot < EDGE

    cells_at = cell_of(lane)
    block_of, lane_of = jnp.where(cells_at < 0, -1, cells_at // LANES), cells_at & (LANES - 1)

    def gather(rows):
        groups = []
        for g in range(rows.shape[0] // 8):
            some = widen(rows[8 * g : 8 * g + 8])
            total = jnp.zeros((8, LANES), rows.dtype)
            for b in range(PADDED // LANES):
                block = jnp.take_along_axis(some[:, LANES * b : LANES * b + LANES], lane_of, axis=1)
                total = jnp.where(block_of == b, block, total)
            groups.append(total)
        return jnp.concatenate(groups, axis=0)

    def spread_rows(values, j):
        return jnp.take_along_axis(values, 2 * j + parity, axis=0)

    for copy in first:
        copy.wait()
    bdepth = gather(lc_ref[...])
    bvd_ref[...] = gather(quads_ref[0].reshape(8 * quad, cells)).reshape(quad, 8, LANES)

    def bcoupling(k):
        if k == 0 or k == levels:
            return jnp.zeros((8, LANES), jnp.float32)
        return jnp.where(k < bdepth, spread_rows(bvd_ref[k % quad], k // quad), 0.0)

    bdif = gather(dif_ref[...])
    along = gather(quads_ref[1].reshape(8 * quad, cells)).reshape(quad, 8, LANES)
    across = gather(quads_ref[2].reshape(8 * quad, cells)).reshape(quad, 8, LANES)
    quarter = 0.25 * bdif
    weight = jnp.where(on_side, bdif, quarter)
    for g in range(quad):
        flow = 0.5 * jnp.where(group < 2, across[g], along[g])
        flow = jnp.where(on_side, jnp.where((group & 1) == 0, flow, -flow), 0.0)
        for j in range(4):
            bflow_ref[quad * j + g] = weight + spread_rows(flow, j)
    code = jnp.zeros((8, LANES), jnp.int32)
    for i in range(2):
        for side in range(4):
            code = jnp.where((parity == i) & (group == side), code_ref[i, side], code)
    turned = jnp.where((code >= 4) & on_side, GROUP * group + (EDGE - 1) - spot, lane)

    middle = levels // 2
    zero = jnp.zeros((8, LANES), jnp.float32)
    coupled = [bcoupling(k) for k in range(levels + 1)]
    inverse, link = [None] * levels, [None] * levels
    excess, low_excess = zero + 1.0, zero + 1.0
    for k in range(middle):
        m = levels - 1 - k
        total, low_total = coupled[k + 1] + excess, coupled[m] + low_excess
        if k < middle - 1:
            inverse[k], inverse[m] = 1.0 / total, 1.0 / low_total
            link[k], link[m] = coupled[k + 1] * inverse[k], coupled[m] * inverse[m]
            excess, low_excess = 1.0 + link[k] * excess, 1.0 + link[m] * low_excess
    joint = coupled[middle]
    meeting = 1.0 / (joint * (excess + low_excess) + excess * low_excess)

    second.wait()
    bcot_ref[...] = gather(cot_ref[...].reshape(8 * levels, cells)).reshape(levels, 8, LANES)
    wide = fetch(
        [
            (source, wide_ref.at[i, :, 2 * n : 2 * n + 2])
            for i, source in enumerate(columns)
            for n in range(4)
        ],
        wide_ref,
    )
    value = [None] * levels
    part, low_part = zero, zero
    for k in range(middle):
        m = levels - 1 - k
        source = bcot_ref[k] + coupled[k] * part
        low_source = bcot_ref[m] + coupled[m + 1] * low_part
        if k < middle - 1:
            part, low_part = source * inverse[k], low_source * inverse[m]
            value[k], value[m] = part, low_part
    value[middle] = (low_source * total + joint * source) * meeting
    value[middle - 1] = (source * low_total + joint * low_source) * meeting
    for k in range(middle - 2, -1, -1):
        m = levels - 1 - k
        value[k] = value[k] + link[k] * value[k + 1]
        value[m] = value[m] + link[m] * value[m - 1]
    for k in range(levels):
        u = jnp.where(k < bdepth, value[k], 0.0)
        diagonal = jnp.where(on_side, quarter * u, 0.0)
        beside = pltpu.roll(diagonal, 1, 1) + pltpu.roll(diagonal, LANES - 1, 1)
        halo = bflow_ref[k] * u + jnp.where(on_side, beside, 0.0)
        strips_ref[k] = jnp.take_along_axis(halo, turned, axis=1)

    lists.wait()
    tile_index = lax.broadcasted_iota(jnp.int32, (2, 4), 0)
    side_index = lax.broadcasted_iota(jnp.int32, (2, 4), 1)
    tables_ref[here] = jnp.zeros((8, LANES), jnp.int32)
    for part_index in range(2):
        tile, kind = lists_ref[2 * part_index], lists_ref[2 * part_index + 1]
        device = tile >> 1
        step = device // PLANE - plane + 1
        step = jnp.where(step < 0, step + planes, step)
        step = jnp.where(step >= planes, step - planes, step)
        slot = PLANE * step + (device & (PLANE - 1))
        slot = jnp.where((tile < 0) | (step > 2), 3 * PLANE, slot)
        swapped = (tile & 1) ^ tile_index
        shift = GROUP * ((side_index - (kind & 3)) & 3)
        tables_ref[here, 2 * part_index : 2 * part_index + 2, 0:4] = slots * swapped + slot
        tables_ref[here, 2 * part_index + 4 : 2 * part_index + 6, 0:4] = shift

    pl.semaphore_wait(barrier, len(peers))

    def send(step, start, some):
        mark = PLANE * (1 - step) + here
        for turn in some:
            pltpu.make_async_remote_copy(
                src_ref=strips_ref.at[pl.ds(chunk * mates[turn], chunk)],
                dst_ref=near_ref.at[mark],
                send_sem=send_sem.at[0],
                recv_sem=recv_sem.at[1 - step],
                device_id={"tile": start + mates[turn]},
                device_id_type=MESH,
            ).start()

    def whole(source, target, mark):
        return pltpu.make_async_remote_copy(
            src_ref=source,
            dst_ref=target,
            send_sem=send_sem.at[SEND_SEMS[mark]],
            recv_sem=recv_sem.at[mark],
            device_id={"tile": own_start + mates[1]},
            device_id_type=MESH,
        )

    @pl.when(low_end == 1)
    def _():
        send(0, own_start, turns[:-1])
        send(leap, leap_start, turns)
        send(-leap, other_start, turns)

    @pl.when(low_end == 0)
    def _():
        send(leap, leap_start, turns)
        send(0, own_start, turns[:-1])
        send(-leap, other_start, turns)

    for turn in turns[:-1]:
        pltpu.make_async_remote_copy(
            src_ref=tables_ref.at[here],
            dst_ref=tables_ref.at[here],
            send_sem=send_sem.at[1],
            recv_sem=recv_sem.at[3],
            device_id={"tile": own_start + mates[turn]},
            device_id_type=MESH,
        ).start()
    near_ref[PLANE + here] = strips_ref[pl.ds(chunk * here, chunk)]
    for slot in (slots - 1, 2 * slots - 1):
        near_ref[slot] = jnp.zeros((chunk, 8, LANES), jnp.float32)

    spots = lax.broadcasted_iota(jnp.int32, (LANES, PADDED), 1)
    cells_at = cell_of(lax.broadcasted_iota(jnp.int32, (LANES, 1), 0))
    placer = jnp.where(spots == cells_at, 1.0, 0.0).astype(jnp.bfloat16)
    pla_ref[0:LANES] = placer
    pla_ref[LANES:] = placer
    wide.wait()
    depth = lc_ref[...]

    def advance(k, state):
        up, excess, part = state
        later = jnp.minimum(k + 1, levels - 1)
        down = jnp.where(k + 1 < depth, wide_ref[0, later], 0.0)
        down = jnp.where(k + 1 < levels, down, 0.0)
        inverse = 1.0 / (down + excess)
        factor = down * inverse
        part = (cot_ref[k] + up * part) * inverse
        factor_ref[k] = factor
        partial_ref[k] = part
        return down, 1.0 + factor * excess, part

    blank = jnp.zeros((8, cells), jnp.float32)
    lax.fori_loop(0, levels, advance, (blank, blank + 1.0, blank), unroll=2)

    wide_lane = lax.broadcasted_iota(jnp.int32, (8, PADDED), 1)
    wraps = PADDED - EDGE
    column = lax.rem(jnp.where(wide_lane >= wraps, wide_lane - wraps, wide_lane), EDGE)
    not_first = column != 0
    not_last = column != EDGE - 1
    diffuse = widen(dif_ref[...])
    quarter_wide = 0.25 * diffuse
    centre = 1.0 - 5.0 * diffuse
    wide_depth = widen(depth)

    def substitute_back(step, solved):
        k = levels - 1 - step
        solved = partial_ref[k] + factor_ref[k] * solved
        u = widen(jnp.where(k < depth, solved, 0.0))
        half_x = 0.5 * widen(wide_ref[1, k])
        half_y = 0.5 * widen(wide_ref[2, k])
        diagonal = quarter_wide * u
        both = pltpu.roll(diagonal, EDGE, 1) + pltpu.roll(diagonal, PADDED - EDGE, 1)
        west = both + (diffuse + half_x) * u
        east = both + (diffuse - half_x) * u
        total = pltpu.roll((diffuse + half_y) * u, PADDED - EDGE, 1)
        total = total + pltpu.roll((diffuse - half_y) * u, EDGE, 1)
        total = total + pltpu.roll(jnp.where(not_first, west, 0.0), PADDED - 1, 1)
        total = total + pltpu.roll(jnp.where(not_last, east, 0.0), 1, 1)
        base_ref[k] = jnp.where(k < wide_depth, centre * u + total, 0.0)
        return solved

    lax.fori_loop(0, levels, substitute_back, blank, unroll=2)

    others = pl.ds(0, PLANE - 1)
    told = whole(tables_ref.at[others], tables_ref.at[others], 3)
    told.wait_recv()
    to_smem = pltpu.make_async_copy(tables_ref, table_smem, in_sem.at[len(used)])
    to_smem.start()

    for below in (1, 2, 0):
        group_slots = PLANE - 1 if below == 1 else PLANE
        some = near_ref.at[pl.ds(PLANE * below, group_slots)]
        whole(some, some, below).wait_recv()
        for slot in range(PLANE * below, PLANE * below + PLANE):
            for t in range(chunk):
                near_ref[slots + slot, t] = jnp.take_along_axis(near_ref[slot, t], row ^ 1, axis=0)
    to_smem.wait()

    chosen = [[(wanted & (group == side))[None] for side in range(4)] for wanted in (on_side, spot == EDGE)]
    for turn in turns:
        pair = []
        for i in range(2):
            total = jnp.zeros((chunk, 8, LANES), jnp.float32)
            for kind in range(2):
                for side in range(4):
                    values = near_ref[table_smem[mates[turn], 2 * kind + i, side]]
                    values = pltpu.roll(values, table_smem[mates[turn], 2 * kind + i + 4, side], 2)
                    total = jnp.where(chosen[kind][side], values, total)
            pair.append(total)
        total = jnp.where((parity == 0)[None], pair[0], pair[1])
        if turn == 0:
            arriving_ref[pl.ds(chunk * here, chunk)] = total
            continue
        picked_ref[turn - 1] = total
        pltpu.make_async_remote_copy(
            src_ref=picked_ref.at[turn - 1],
            dst_ref=arriving_ref.at[pl.ds(chunk * here, chunk)],
            send_sem=send_sem.at[2],
            recv_sem=recv_sem.at[PICK_SEMS[turn]],
            device_id={"tile": own_start + mates[turn]},
            device_id_type=MESH,
        ).start()

    for members in PICK_GROUPS:
        some = arriving_ref.at[pl.ds(0, chunk * len([turn for turn in members if turn]))]
        whole(some, some, PICK_SEMS[members[-1]]).wait_recv()
        places = [chunk * mates[turn] + t for turn in members for t in range(chunk)]
        rows = [jnp.where(k < bdepth, arriving_ref[k], 0.0) for k in places]
        high, low = halves(jnp.concatenate(rows, axis=0))
        returned = jnp.dot(
            jnp.concatenate([high, low], axis=1), pla_ref[...], preferred_element_type=jnp.float32
        )
        for n, k in enumerate(places):
            result = base_ref[k] + returned[8 * n : 8 * n + 8]
            out_ref[k] = result[:, :cells]
    every = near_ref.at[pl.ds(0, 3 * PLANE - 1)]
    whole(every, every, 0).wait_send()
    told.wait_send()
    whole(picked_ref, picked_ref, 4).wait_send()


def store_kernel(held_ref, out_hbm, sem):
    for n in range(4):
        pltpu.make_async_copy(held_ref.at[:, 2 * n : 2 * n + 2], out_hbm.at[:, n], sem).start()
    pltpu.make_async_copy(out_hbm, out_hbm, sem).wait()


def shards_fast(
    cotangent,
    courant_x,
    courant_y,
    diffusivity,
    vert_diff,
    level_count,
    edge_tile,
    edge_code,
    corner_tile,
    corner_code,
):
    levels, tracers, tiles_here, cells = cotangent.shape
    count = lax.axis_size("tile")
    vmem = pl.BlockSpec(memory_space=pltpu.VMEM)
    hbm = pl.BlockSpec(memory_space=pltpu.HBM)
    chunk = levels // PLANE
    f32 = jnp.float32
    held = pl.pallas_call(
        functools.partial(exchange_kernel, count),
        name="exchange",
        out_shape=pltpu.VMEM((levels, 8, cells), f32),
        in_specs=[hbm] * 10,
        out_specs=vmem,
        scratch_shapes=[
            pltpu.VMEM((levels, 8, cells), f32),
            pltpu.VMEM((3, levels // 4, 8, cells), f32),
            pltpu.VMEM((8, cells), f32),
            pltpu.VMEM((8, cells), jnp.int32),
            pltpu.VMEM((3, levels, 8, cells), f32),
            pltpu.VMEM((4, 2, 4), jnp.int32),
            pltpu.SMEM((2, 4), jnp.int32),
            pltpu.VMEM((2 * LANES, PADDED), jnp.bfloat16),
            pltpu.VMEM((levels, 8, LANES), f32),
            pltpu.VMEM((levels // 4, 8, LANES), f32),
            pltpu.VMEM((levels, 8, LANES), f32),
            pltpu.VMEM((levels, 8, LANES), f32),
            pltpu.VMEM((levels, 8, cells), f32),
            pltpu.VMEM((levels, 8, cells), f32),
            pltpu.VMEM((levels, 8, PADDED), f32),
            pltpu.VMEM((PLANE, 8, LANES), jnp.int32),
            pltpu.SMEM((PLANE, 8, LANES), jnp.int32),
            pltpu.VMEM((2 * (3 * PLANE + 1), chunk, 8, LANES), f32),
            pltpu.VMEM((PLANE - 1, chunk, 8, LANES), f32),
            pltpu.VMEM((levels, 8, LANES), f32),
            pltpu.SemaphoreType.DMA((8,)),
            pltpu.SemaphoreType.DMA((3,)),
            pltpu.SemaphoreType.DMA((7,)),
        ],
        compiler_params=pltpu.CompilerParams(
            collective_id=0, has_side_effects=True, vmem_limit_bytes=62 << 20
        ),
    )(
        cotangent, courant_x, courant_y, diffusivity, vert_diff, level_count,
        edge_tile, edge_code, corner_tile, corner_code,
    )
    return pl.pallas_call(
        store_kernel,
        name="store",
        out_shape=jax.ShapeDtypeStruct(cotangent.shape, f32),
        in_specs=[vmem],
        out_specs=hbm,
        scratch_shapes=[pltpu.SemaphoreType.DMA],
        compiler_params=pltpu.CompilerParams(vmem_limit_bytes=8 << 20),
    )(held)


def solution(mesh):
    placed = (
        P("lev", None, "tile", None),
        P("lev", "tile", None),
        P("lev", "tile", None),
        P("tile", None),
        P("lev", "tile", None),
        P("tile", None),
        P("tile", None),
        P("tile", None),
        P("tile", None),
        P("tile", None),
    )
    fast = mesh.shape["lev"] == 1 and mesh.shape["tile"] % PLANE == 0 and mesh.shape["tile"] > 2 * BAND
    return jax.shard_map(
        shards_fast if fast else shards, mesh=mesh, in_specs=placed, out_specs=P("lev", None, "tile", None), check_vma=False
    )
```
